32 devices in a mesh: ves: 16 (over z, y, x), sec: 2 (over core).
Axes of the slice: x: 2, y: 2, z: 4, core: 2. Of those that a mesh axis runs over, the one named last changes fastest.
Arguments:
- density: bfloat16 [8192, 3, 544], P(('ves', 'sec')), may hold values from -6 to 6
- analysis: bfloat16 [544, 289], replicated, may hold values from -0.25 to 0.25
- synthesis: bfloat16 [289, 544], replicated, may hold values from -0.375 to 0.375
- degree_gain: float32 [289], replicated, may hold values from 0.05 to 2
- near_kernel: bfloat16 [544, 544], replicated, may hold values from -0.25 to 0.25
- partners: int32 [8192, 4], P(('ves', 'sec')), may hold values from 0 to 8191, as said below
- pair_weight: float32 [8192, 4], P(('ves', 'sec')), may hold values from 0.2 to 1
- wall_list: int32 [512], P(('ves', 'sec')), may hold values from 0 to 8191, as said below
- coupling: bfloat16 [4096, 32], P(('ves', 'sec')), may hold values from -1 to 1
- wall_gain: float32 [4096], P(('ves', 'sec')), may hold values from 0.5 to 2
Outputs:
- velocity: float32 [8192, 3, 544], P(('ves', 'sec'))
The draws below stay inside these ranges and needn't reach their ends.
Inputs may be any that keep to these rules, and one draw needn't show every extreme that they name: `partners`: vesicles form blocks of 256 consecutive ids, block b in region b // 2, slot b % 2. A partner of vesicle i lies in the block of i, or among the last 64 vesicles of the block of the region below with the same slot, or among the first 64 of the block of the region above with the same slot. No vesicle is its own partner. `wall_list`: entry block b (entries b * 16 to b * 16 + 15) holds 16 distinct ids of vesicle block b.
All inputs are finite; a program needn't handle non-finite values.
Results may differ from the reference program's by a relative error of at most 0.0043.
Values may be sent and summed in bfloat16 or wider, within the bound.
A program may use at most 64 MiB of HBM per device.

```python
import math
import jax
import jax.numpy as jnp
from jax import lax

P_SIZE = 544
L = 289
K = 4
V_DEV = 256
NW_DEV = 16
Q_DEV = 128
H = 64
V = 8192
NWREG = 32
NQ = 4096
NWALL = 512
N_VES = 16
N_SEC = 2


def draw_partners(key, part):
    index = jnp.arange(V, dtype=jnp.int32)
    block = index // V_DEV
    local = (index % V_DEV)[:, None]
    region = (block // N_SEC)[:, None]
    slot = (block % N_SEC)[:, None]
    window = jax.random.randint(key, (V, K), 0, V_DEV + 2 * H, dtype=jnp.int32)
    window = jnp.where((region == 0) & (window < H), window + H, window)
    window = jnp.where((region == N_VES - 1) & (window >= V_DEV + H), window - H, window)
    window = jnp.where(window - H == local, H + (local + 1) % V_DEV, window)
    shift = jnp.where(window < H, -1, jnp.where(window >= V_DEV + H, 1, 0))
    inner = jnp.where(shift == -1, window + V_DEV - H, jnp.where(shift == 1, window - H - V_DEV, window - H))
    target = (region + shift) * N_SEC + slot
    return (target * V_DEV + inner).astype(jnp.int32)


def draw_wall_list(key, part):
    blocks = V // V_DEV
    keys = jax.random.split(key, blocks)
    chosen = jax.vmap(lambda one_key: jax.random.permutation(one_key, V_DEV)[:NW_DEV])(keys)
    chosen = chosen.astype(jnp.int32) + (jnp.arange(blocks, dtype=jnp.int32) * V_DEV)[:, None]
    return chosen.reshape(-1).astype(jnp.int32)


def shard_levels(stream_key, extent, pieces, low, top_value):
    loudness, own = 1.0, jax.random.fold_in(stream_key, 6)
    for axis_at, blocks in pieces:
        steps = jnp.exp(jax.random.uniform(jax.random.fold_in(own, axis_at), (blocks,), jnp.float32, low / len(pieces), top_value / len(pieces)))
        loudness = loudness * jnp.repeat(steps, extent[axis_at] // blocks).reshape([-1 if axis == axis_at else 1 for axis in range(len(extent))])
    return loudness


def normal_values(own_key, shape, deviation, limit, cuts=(), kind=jnp.bfloat16):
    loudness = shard_levels(own_key, shape, cuts, -0.22, 0.18) if cuts else 1.0
    entries = jax.random.normal(own_key, shape, jnp.float32) * deviation * loudness
    return jnp.minimum(jnp.maximum(entries, -limit), limit).astype(kind)


def setup_inputs(seed: int = 0) -> dict:
    seeds = jax.random.split(jax.random.key(seed), 11)
    density = normal_values(seeds[0], (V, 3, P_SIZE), 1.0, 6.0, ((0, 32),))
    analysis = normal_values(seeds[1], (P_SIZE, L), P_SIZE ** -0.5, 0.25)
    synthesis = normal_values(seeds[2], (L, P_SIZE), L ** -0.5, 0.375)
    degree_gain = jnp.clip(jnp.exp(jax.random.uniform(seeds[3], (L,), jnp.float32, math.log(0.05), math.log(2.0))), 0.05, 2.0)
    near_kernel = normal_values(seeds[4], (P_SIZE, P_SIZE), P_SIZE ** -0.5, 0.25)
    partners = draw_partners(jax.random.fold_in(seeds[10], 71), 0)
    pair_weight = jnp.clip(0.2 + 0.8 * jax.random.uniform(seeds[6], (V, K), jnp.float32) ** shard_levels(seeds[6], (V, K), ((0, 32),), -0.2, 0.2), 0.2, 1.0)
    wall_list = draw_wall_list(jax.random.fold_in(seeds[10], 71), 0)
    coupling = normal_values(seeds[8], (NQ, NWREG), NWREG ** -0.5, 1.0, ((0, 32),))
    wall_gain = jnp.clip(jnp.exp(math.log(2.0) - 1.3862944 * jax.random.uniform(seeds[9], (NQ,), jnp.float32) ** shard_levels(seeds[9], (NQ,), ((0, 32),), -0.2, 0.2)), 0.5, 2.0)
    return dict(density=density, analysis=analysis, synthesis=synthesis, degree_gain=degree_gain, near_kernel=near_kernel, partners=partners, pair_weight=pair_weight, wall_list=wall_list, coupling=coupling, wall_gain=wall_gain)


def reference(density, analysis, synthesis, degree_gain, near_kernel, partners, pair_weight, wall_list, coupling, wall_gain):
    blocks = V // V_DEV
    dens = density.reshape(blocks, V_DEV * 3, P_SIZE)

    def first(block_dens):
        coef = jnp.dot(block_dens, analysis, preferred_element_type=jnp.float32).astype(jnp.bfloat16)
        smooth = jnp.dot(coef, synthesis, preferred_element_type=jnp.float32).astype(jnp.bfloat16)
        return coef, smooth

    coef, smooth = lax.map(first, dens)
    smooth_flat = smooth.reshape(V, 3, P_SIZE)
    coef_flat = coef.reshape(V, 3 * L)
    region_ids = wall_list.reshape(N_VES, NWREG)
    region_g = coupling.reshape(N_VES, Q_DEV * N_SEC, NWREG)
    region_gain = wall_gain.reshape(N_VES, Q_DEV * N_SEC)

    def wall(args):
        ids, gmat, gain = args
        xmat = coef_flat[ids]
        wall_dens = (gain[:, None] * jnp.dot(gmat, xmat, preferred_element_type=jnp.float32)).astype(jnp.bfloat16)
        back = jnp.dot(gmat.T, wall_dens, preferred_element_type=jnp.float32)
        return back.astype(jnp.bfloat16)

    backs = lax.map(wall, (region_ids, region_g, region_gain))
    wall_coef = jnp.zeros((V, 3 * L), jnp.bfloat16).at[wall_list].set(backs.reshape(NWALL, 3 * L))

    def second(args):
        block_coef, ids, weights, wcoef = args
        scaled = (block_coef.astype(jnp.float32) * degree_gain).astype(jnp.bfloat16)
        self_vel = jnp.dot(scaled, synthesis, preferred_element_type=jnp.float32)
        gathered = smooth_flat[ids]
        mixed = jnp.zeros((V_DEV, 3, P_SIZE), jnp.float32)
        for k in range(K):
            mixed = mixed + weights[:, k, None, None] * gathered[:, k].astype(jnp.float32)
        mixed = mixed.astype(jnp.bfloat16).reshape(V_DEV * 3, P_SIZE)
        near_vel = jnp.dot(mixed, near_kernel, preferred_element_type=jnp.float32)
        wall_vel = jnp.dot(wcoef, synthesis, preferred_element_type=jnp.float32)
        return self_vel + near_vel + wall_vel

    out = lax.map(second, (coef, partners.reshape(blocks, V_DEV, K), pair_weight.reshape(blocks, V_DEV, K), wall_coef.reshape(blocks, V_DEV * 3, L)))
    return out.reshape(V, 3, P_SIZE)
```

```python
import functools

import jax
import jax.numpy as jnp
from jax import lax
from jax.experimental import pallas as pl
from jax.experimental.pallas import tpu as pltpu
from jax.sharding import PartitionSpec as P

MESH = pl.DeviceIdType.MESH
F32 = jnp.float32
BF16 = jnp.bfloat16


def dot(a, b, ca=1, cb=0):
    return lax.dot_general(a, b, (((ca,), (cb,)), ((), ())), preferred_element_type=F32)


def step_kernel(
    n_ves,
    n_sec,
    dens_in,
    ana_in,
    syn_in,
    gain_in,
    near_in,
    part_in,
    weight_in,
    list_in,
    coup_in,
    wgain_in,
    out_ref,
    dens_ref,
    ana_ref,
    syn_ref,
    near_ref,
    part_ref,
    weight_ref,
    list_ref,
    coup_ref,
    wgain_ref,
    gain_ref,
    syn_turned,
    both_ref,
    load_sem,
    coef_ref,
    mix_ref,
    total_ref,
    tail_ref,
    head_ref,
    recv_ref,
    pick_all,
    coup_all,
    gain_all,
    send_sem,
    recv_sem,
    wall_send,
    wall_recv,
):
    ves = lax.axis_index("ves")
    sec = lax.axis_index("sec")
    comps, _, count = dens_ref.shape
    num_coefs = ana_ref.shape[0]
    near_wall = list_ref.shape[0]
    edge = count // 4
    tile = 2 * edge
    cut = recv_ref.shape[2]
    top = num_coefs - cut
    has_left = ves > 0
    has_right = ves < n_ves - 1
    hops = range(1, n_sec)

    barrier = pltpu.get_barrier_semaphore()

    @pl.when(has_left)
    def _():
        pl.semaphore_signal(barrier, inc=1, device_id=(ves - 1, sec), device_id_type=MESH)

    @pl.when(has_right)
    def _():
        pl.semaphore_signal(barrier, inc=1, device_id=(ves + 1, sec), device_id_type=MESH)

    for hop in hops:
        peer = lax.rem(sec + hop, n_sec)
        pl.semaphore_signal(barrier, inc=1, device_id=(ves, peer), device_id_type=MESH)

    pairs = [(ana_in, ana_ref)]
    pairs += [(dens_in.at[c], dens_ref.at[c]) for c in range(comps)]
    pairs += [
        (list_in, list_ref),
        (part_in, part_ref),
        (weight_in, weight_ref),
        (coup_in, coup_ref),
        (wgain_in, wgain_ref),
        (gain_in, gain_ref),
        (syn_in, syn_ref),
        (near_in, near_ref),
    ]
    loads = [
        pltpu.make_async_copy(src, dst, load_sem.at[i]) for i, (src, dst) in enumerate(pairs)
    ]
    for load in loads[:-2]:
        load.start()
    load_ana, *load_dens = loads[: comps + 1]
    load_list, load_part, load_weight, load_coup, load_wgain, load_gain, load_syn, load_near = loads[comps + 1 :]

    def halo_copy(src, side, c, to):
        return pltpu.make_async_remote_copy(
            src_ref=src.at[c],
            dst_ref=recv_ref.at[side, c],
            send_sem=send_sem.at[side, c],
            recv_sem=recv_sem.at[side, c],
            device_id=(to, sec),
            device_id_type=MESH,
        )

    def up_copy(c):
        return halo_copy(tail_ref, 0, c, ves + 1)

    def down_copy(c):
        return halo_copy(head_ref, 1, c, ves - 1)

    def wall_copy(hop, kind):
        src, dst = (
            (coup_in, coup_all.at[hop - 1]),
            (wgain_in, gain_all.at[hop - 1]),
            (pick_all.at[sec], pick_all.at[sec]),
        )[kind]
        return pltpu.make_async_remote_copy(
            src_ref=src,
            dst_ref=dst,
            send_sem=wall_send.at[kind, hop - 1],
            recv_sem=wall_recv.at[kind, hop - 1],
            device_id=(ves, lax.rem(sec + hop, n_sec)),
            device_id_type=MESH,
        )

    @pl.when(jnp.logical_not(has_left))
    def _():
        recv_ref[0] = jnp.zeros(recv_ref.shape[1:], BF16)

    @pl.when(jnp.logical_not(has_right))
    def _():
        recv_ref[1] = jnp.zeros(recv_ref.shape[1:], BF16)

    low = lax.broadcasted_iota(jnp.int32, (cut, tile), 1) < edge
    load_ana.wait()
    ana = ana_ref[...]

    far_up = lax.rem(ves, 2) == 1
    up_first = ves != 1

    def send_up(c, cond):
        @pl.when(jnp.logical_and(has_right, cond))
        def _():
            up_copy(c).start()

    def send_down(c, cond):
        @pl.when(jnp.logical_and(has_left, cond))
        def _():
            down_copy(c).start()

    def greet():
        sides = has_left.astype(jnp.int32) + has_right.astype(jnp.int32)
        pl.semaphore_wait(barrier, n_sec - 1 + sides)

    for c in range(comps):
        load_dens[c].wait()
        full = dot(ana, dens_ref[c])
        coef_ref[c] = full.astype(BF16)
        head = full[:, :tile]
        tail = full[:, count - tile :]
        tail_ref[c] = jnp.where(low, pltpu.roll(tail, edge, 1)[:cut], tail[top:]).astype(BF16)
        head_ref[c] = jnp.where(low, head[:cut], pltpu.roll(head, edge, 1)[top:]).astype(BF16)
        if c == 0:
            @pl.when(has_left)
            def _():
                greet()
            load_syn.start()
            load_near.start()
        send_up(c, jnp.logical_and(up_first, has_left))
        send_down(c, True)

    @pl.when(jnp.logical_not(has_left))
    def _():
        greet()

    for c in range(comps):
        send_up(c, jnp.logical_not(up_first))
    for c in range(comps):
        @pl.when(jnp.logical_not(has_left))
        def _():
            up_copy(c).start()

    for hop in hops:
        wall_copy(hop, 0).start()
        wall_copy(hop, 1).start()

    base = (ves * n_sec + sec) * count

    def placing(rows, first):
        row = lax.broadcasted_iota(jnp.int32, (rows, count), 0)
        ids = jnp.full((rows, count), -1, jnp.int32)
        for j in range(near_wall):
            ids = jnp.where(row == first + j, list_ref[j] - base, ids)
        hit = ids == lax.broadcasted_iota(jnp.int32, (rows, count), 1)
        return jnp.where(hit, 1.0, 0.0).astype(BF16)

    load_list.wait()
    choose = placing(near_wall, 0)
    for c in range(comps):
        pick_all[sec, c] = dot(choose, coef_ref[c], 1, 1).astype(BF16)
    for hop in hops:
        wall_copy(hop, 2).start()

    load_part.wait()
    load_weight.wait()
    shift = part_ref[...] - base
    weight = weight_ref[...]

    def mixing(rows, start):
        want = lax.broadcasted_iota(jnp.int32, (rows, count), 0) + start
        total = jnp.zeros((rows, count), F32)
        for k in range(shift.shape[0]):
            total = total + jnp.where(shift[k : k + 1, :] == want, weight[k : k + 1, :], 0.0)
        return total.astype(BF16)

    own_mix = mixing(count, 0)
    left_mix = mixing(edge, count - edge - n_sec * count)
    right_mix = mixing(edge, n_sec * count)
    none = jnp.zeros((edge, count), BF16)
    first_mix = jnp.concatenate([left_mix, none, right_mix, none], axis=0)
    second_mix = jnp.concatenate([none, left_mix, none, right_mix], axis=0)

    load_gain.wait()
    square = (num_coefs, num_coefs)
    diagonal = lax.broadcasted_iota(jnp.int32, square, 0) == lax.broadcasted_iota(
        jnp.int32, square, 1
    )
    gain = jnp.sum(jnp.where(diagonal, gain_ref[...].reshape(1, num_coefs), 0.0), axis=1, keepdims=True)

    for c in range(comps):
        mix_ref[c] = dot(coef_ref[c], own_mix)

    load_syn.wait()
    syn_turned[...] = syn_ref[...].T
    syn = syn_turned[...]
    load_near.wait()
    both_ref[...] = dot(near_ref[...].T, syn).astype(BF16)

    for hop in hops:
        for kind in range(3):
            wall_copy(hop, kind).wait()
    load_coup.wait()
    load_wgain.wait()
    coup = jnp.concatenate([coup_ref[...]] + [coup_all[hop - 1] for hop in hops], axis=1)
    wgain = jnp.concatenate([wgain_ref[...]] + [gain_all[hop - 1] for hop in hops], axis=1)
    place = placing(near_wall * n_sec, sec * near_wall)
    for c in range(comps):
        picked = jnp.concatenate([pick_all[s, c] for s in range(n_sec)], axis=0)
        dens = (dot(picked, coup, 0, 0) * wgain).astype(BF16)
        back = dot(coup, dens, 1, 1).astype(BF16)
        wall = dot(back, place, 0, 0)
        scaled = coef_ref[c].astype(F32) * gain
        out_ref[c] = dot(syn, (scaled + wall).astype(BF16))

    def receive(c):
        @pl.when(has_left)
        def _():
            up_copy(c).wait_recv()

        @pl.when(has_right)
        def _():
            down_copy(c).wait_recv()

    for c in range(comps):
        receive(c)
        halo = jnp.concatenate([recv_ref[0, c], recv_ref[1, c]], axis=1)
        first = dot(halo[:top], first_mix)
        second = dot(halo, second_mix)
        total_ref[:top] = (mix_ref[c, :top] + first).astype(BF16)
        total_ref[top:] = (mix_ref[c, top:] + second).astype(BF16)
        total = total_ref[...]
        out_ref[c] = out_ref[c] + dot(both_ref[...], total)

    for c in range(comps):

        @pl.when(has_right)
        def _():
            up_copy(c).wait_send()

        @pl.when(has_left)
        def _():
            down_copy(c).wait_send()


def shards(
    n_ves,
    n_sec,
    density,
    analysis,
    synthesis,
    degree_gain,
    near_kernel,
    partners,
    pair_weight,
    wall_list,
    coupling,
    wall_gain,
):
    count, comps, num_points = density.shape
    num_coefs = analysis.shape[1]
    near_wall = wall_list.shape[0]
    panels, region_wall = coupling.shape
    tile = count // 2
    top = num_coefs // 2 // 16 * 16
    cut = num_coefs - top
    others = max(n_sec - 1, 1)
    vmem = pl.BlockSpec(memory_space=pltpu.VMEM)
    specs = [pl.BlockSpec(memory_space=pltpu.HBM)] * 10
    out = pl.pallas_call(
        functools.partial(step_kernel, n_ves, n_sec),
        name="vesicle_step",
        out_shape=jax.ShapeDtypeStruct((comps, num_points, count), F32),
        in_specs=specs,
        out_specs=vmem,
        scratch_shapes=[
            pltpu.VMEM((comps, num_points, count), BF16),
            pltpu.VMEM((num_coefs, num_points), BF16),
            pltpu.VMEM((num_coefs, num_points), BF16),
            pltpu.VMEM((num_points, num_points), BF16),
            pltpu.VMEM(partners.shape[::-1], jnp.int32),
            pltpu.VMEM(partners.shape[::-1], F32),
            pltpu.SMEM((near_wall,), jnp.int32),
            pltpu.VMEM((region_wall, panels), BF16),
            pltpu.VMEM((1, panels), F32),
            pltpu.VMEM((num_coefs,), F32),
            pltpu.VMEM((num_points, num_coefs), BF16),
            pltpu.VMEM((num_points, num_coefs), BF16),
            pltpu.SemaphoreType.DMA((comps + 9,)),
            pltpu.VMEM((comps, num_coefs, count), BF16),
            pltpu.VMEM((comps, num_coefs, count), F32),
            pltpu.VMEM((num_coefs, count), BF16),
            pltpu.VMEM((comps, cut, tile), BF16),
            pltpu.VMEM((comps, cut, tile), BF16),
            pltpu.VMEM((2, comps, cut, tile), BF16),
            pltpu.VMEM((n_sec, comps, near_wall, num_coefs), BF16),
            pltpu.VMEM((others, region_wall, panels), BF16),
            pltpu.VMEM((others, 1, panels), F32),
            pltpu.SemaphoreType.DMA((2, comps)),
            pltpu.SemaphoreType.DMA((2, comps)),
            pltpu.SemaphoreType.DMA((3, others)),
            pltpu.SemaphoreType.DMA((3, others)),
        ],
        compiler_params=pltpu.CompilerParams(
            collective_id=0, has_side_effects=True, vmem_limit_bytes=32 * 1024 * 1024
        ),
    )(
        *(
            pltpu.with_memory_space_constraint(array, pltpu.HBM)
            for array in (
                density.transpose(1, 2, 0),
                analysis.T,
                synthesis,
                degree_gain,
                near_kernel,
                partners.T,
                pair_weight.T,
                wall_list,
                coupling.T,
                wall_gain.reshape(1, panels),
            )
        )
    )
    return out.transpose(2, 0, 1)


def solution(mesh):
    n_ves, n_sec = mesh.shape["ves"], mesh.shape["sec"]
    return jax.shard_map(
        functools.partial(shards, n_ves, n_sec),
        mesh=mesh,
        in_specs=(
            P(("ves", "sec"), None, None),
            P(),
            P(),
            P(),
            P(),
            P(("ves", "sec"), None),
            P(("ves", "sec"), None),
            P(("ves", "sec")),
            P(("ves", "sec"), None),
            P(("ves", "sec")),
        ),
        out_specs=P(("ves", "sec"), None, None),
        check_vma=False,
    )
```

```python
import functools

import jax
import jax.numpy as jnp
from jax import lax
from jax.experimental import pallas as pl
from jax.experimental.pallas import tpu as pltpu
from jax.sharding import PartitionSpec as P

MESH = pl.DeviceIdType.MESH
F32 = jnp.float32
BF16 = jnp.bfloat16


def dot(a, b, ca=1, cb=0):
    return lax.dot_general(a, b, (((ca,), (cb,)), ((), ())), preferred_element_type=F32)


def dot_rows(a, b, cut):
    return jnp.concatenate([dot(a[:cut], b), dot(a[cut:], b)], axis=0)


def halo_mix(recv_ref, spread_ref, c, top):
    halo = jnp.concatenate([recv_ref[0, c], recv_ref[1, c]], axis=1)
    return dot(halo[:top], spread_ref[0]), dot(halo, spread_ref[1])


def step_kernel(
    n_ves,
    n_sec,
    dens_in,
    ana_in,
    syn_in,
    gain_in,
    near_in,
    part_in,
    weight_in,
    list_in,
    coup_in,
    wgain_in,
    out_ref,
    both_ref,
    mix_ref,
    total_ref,
    spread_ref,
    recv_ref,
    dens_ref,
    ana_ref,
    syn_ref,
    near_ref,
    part_ref,
    weight_ref,
    list_ref,
    coup_ref,
    wgain_ref,
    gain_ref,
    syn_turned,
    coef_ref,
    tail_ref,
    head_ref,
    pick_all,
    coup_all,
    gain_all,
    send_sem,
    recv_sem,
    wall_recv,
):
    ves = lax.axis_index("ves")
    sec = lax.axis_index("sec")
    comps, _, count = dens_ref.shape
    num_coefs = ana_ref.shape[0]
    near_wall = list_ref.shape[0]
    edge = count // 4
    tile = 2 * edge
    cut = recv_ref.shape[2]
    top = num_coefs - cut
    half = out_ref.shape[1] // 2
    has_left = ves > 0
    has_right = ves < n_ves - 1
    hops = range(1, n_sec)

    barrier = pltpu.get_barrier_semaphore()

    @pl.when(has_left)
    def _():
        pl.semaphore_signal(barrier, inc=1, device_id=(ves - 1, sec), device_id_type=MESH)

    @pl.when(has_right)
    def _():
        pl.semaphore_signal(barrier, inc=1, device_id=(ves + 1, sec), device_id_type=MESH)

    for hop in hops:
        peer = lax.rem(sec + hop, n_sec)
        pl.semaphore_signal(barrier, inc=1, device_id=(ves, peer), device_id_type=MESH)

    def halo_copy(src, side, part, to):
        return pltpu.make_async_remote_copy(
            src_ref=src.at[part],
            dst_ref=recv_ref.at[side, part],
            send_sem=send_sem.at[side],
            recv_sem=recv_sem.at[side, part],
            device_id=(to, sec),
            device_id_type=MESH,
        )

    def up_copy(c):
        return halo_copy(tail_ref, 0, c, ves + 1)

    def down_copy(c):
        return halo_copy(head_ref, 1, c, ves - 1)

    turn = lax.rem(ves, 4)
    up_first = (turn == 0)
    greet_stage = jnp.where(ves == 0, jnp.where(sec == 0, 4, 2), jnp.where(turn == 0, 2, jnp.where(turn == 1, 0, jnp.where(turn == 2, 0, 0))))
    second_stage = jnp.where(ves == 0, jnp.where(sec == 0, 4, 3), jnp.where(turn == 0, 5, jnp.where(turn == 1, jnp.where(sec == 0, 2, 4), jnp.where(turn == 2, 3, 3))))

    def send(c, lead, when):
        up = up_first if lead else jnp.logical_not(up_first)

        @pl.when(when & has_right & up)
        def _():
            up_copy(c).start()

        @pl.when(when & has_left & jnp.logical_not(up))
        def _():
            down_copy(c).start()

    def at_stage(stage):
        @pl.when(greet_stage == stage)
        def _():
            sides = has_left.astype(jnp.int32) + has_right.astype(jnp.int32)
            pl.semaphore_wait(barrier, n_sec - 1 + sides)

        for c in range(comps):
            if c == stage:
                send(c, True, greet_stage <= stage)
            elif c < stage:
                send(c, True, greet_stage == stage)
        if stage >= comps - 1:
            for c in range(comps):
                send(c, False, second_stage == stage)

    def work(load_sem, wall_send):
        pairs = [(ana_in, ana_ref)]
        pairs += [(dens_in.at[c], dens_ref.at[c]) for c in range(comps)]
        pairs += [
            (list_in, list_ref),
            (part_in, part_ref),
            (weight_in, weight_ref),
            (coup_in, coup_ref),
            (wgain_in, wgain_ref),
            (gain_in, gain_ref),
            (syn_in, syn_ref),
            (near_in, near_ref),
        ]
        loads = [
            pltpu.make_async_copy(src, dst, load_sem.at[i]) for i, (src, dst) in enumerate(pairs)
        ]
        for load in loads[:-2]:
            load.start()
        load_ana, *load_dens = loads[: comps + 1]
        load_list, load_part, load_weight, load_coup, load_wgain, load_gain, load_syn, load_near = (
            loads[comps + 1 :]
        )

        def wall_copy(hop, kind):
            src, dst = (
                (coup_in, coup_all.at[hop - 1]),
                (wgain_in, gain_all.at[hop - 1]),
                (pick_all.at[sec], pick_all.at[sec]),
            )[kind]
            return pltpu.make_async_remote_copy(
                src_ref=src,
                dst_ref=dst,
                send_sem=wall_send.at[kind, hop - 1],
                recv_sem=wall_recv.at[kind, hop - 1],
                device_id=(ves, lax.rem(sec + hop, n_sec)),
                device_id_type=MESH,
            )

        def send_walls(when):
            @pl.when(when)
            def _():
                for hop in hops:
                    for kind in (2, 0, 1):
                        wall_copy(hop, kind).start()

        @pl.when(jnp.logical_not(has_left))
        def _():
            recv_ref[0] = jnp.zeros(recv_ref.shape[1:], BF16)

        @pl.when(jnp.logical_not(has_right))
        def _():
            recv_ref[1] = jnp.zeros(recv_ref.shape[1:], BF16)

        low = lax.broadcasted_iota(jnp.int32, (cut, tile), 1) < edge
        load_ana.wait()
        ana = ana_ref[...]

        for c in range(comps):
            load_dens[c].wait()
            full = dot_rows(ana, dens_ref[c], top)
            coef_ref[c] = full.astype(BF16)
            head = full[:, :tile]
            tail = full[:, count - tile :]
            tail_ref[c] = jnp.where(low, pltpu.roll(tail, edge, 1)[:cut], tail[top:]).astype(BF16)
            head_ref[c] = jnp.where(low, head[:cut], pltpu.roll(head, edge, 1)[top:]).astype(BF16)
            if c == 0:
                load_syn.start()
                load_near.start()
            at_stage(c)

        base = (ves * n_sec + sec) * count

        def placing(rows, first):
            row = lax.broadcasted_iota(jnp.int32, (rows, count), 0)
            ids = jnp.full((rows, count), -1, jnp.int32)
            for j in range(near_wall):
                ids = jnp.where(row == first + j, list_ref[j] - base, ids)
            hit = ids == lax.broadcasted_iota(jnp.int32, (rows, count), 1)
            return jnp.where(hit, 1.0, 0.0).astype(BF16)

        load_list.wait()
        choose = placing(near_wall, 0)
        for c in range(comps):
            pick_all[sec, c] = dot(choose, coef_ref[c], 1, 1).astype(BF16)
        at_stage(comps)
        send_walls(greet_stage <= comps)

        load_part.wait()
        load_weight.wait()
        shift = part_ref[...] - base
        weight = weight_ref[...]

        def mixing(rows, start):
            want = lax.broadcasted_iota(jnp.int32, (rows, count), 0) + start
            total = jnp.zeros((rows, count), F32)
            for k in range(shift.shape[0]):
                total = total + jnp.where(shift[k : k + 1, :] == want, weight[k : k + 1, :], 0.0)
            return total.astype(BF16)

        own_mix = mixing(count, 0)
        left_mix = mixing(edge, count - edge - n_sec * count)
        right_mix = mixing(edge, n_sec * count)
        none = jnp.zeros((edge, count), BF16)
        spread_ref[0] = jnp.concatenate([left_mix, none, right_mix, none], axis=0)
        spread_ref[1] = jnp.concatenate([none, left_mix, none, right_mix], axis=0)

        load_gain.wait()
        square = (num_coefs, num_coefs)
        diagonal = lax.broadcasted_iota(jnp.int32, square, 0) == lax.broadcasted_iota(
            jnp.int32, square, 1
        )
        gain = jnp.sum(
            jnp.where(diagonal, gain_ref[...].reshape(1, num_coefs), 0.0), axis=1, keepdims=True
        )

        for c in range(comps):
            mix_ref[c] = dot(coef_ref[c], own_mix)
        at_stage(comps + 1)
        send_walls(greet_stage > comps)

        load_syn.wait()
        syn_turned[...] = syn_ref[...].T
        syn = syn_turned[...]
        load_near.wait()
        both_ref[...] = dot(near_ref[...].T, syn).astype(BF16)
        at_stage(comps + 2)

        for hop in hops:
            for kind in range(3):
                wall_copy(hop, kind).wait()
        load_coup.wait()
        load_wgain.wait()
        coup = jnp.concatenate([coup_ref[...]] + [coup_all[hop - 1] for hop in hops], axis=1)
        wgain = jnp.concatenate([wgain_ref[...]] + [gain_all[hop - 1] for hop in hops], axis=1)
        place = placing(near_wall * n_sec, sec * near_wall)
        for c in range(comps):
            picked = jnp.concatenate([pick_all[s, c] for s in range(n_sec)], axis=0)
            dens = (dot(picked, coup, 0, 0) * wgain).astype(BF16)
            back = dot(coup, dens, 1, 1).astype(BF16)
            wall = dot(back, place, 0, 0)
            scaled = coef_ref[c].astype(F32) * gain
            out_ref[c] = dot_rows(syn, (scaled + wall).astype(BF16), half)

    pl.run_scoped(
        work,
        pltpu.SemaphoreType.DMA((comps + 9,)),
        pltpu.SemaphoreType.DMA((3, max(n_sec - 1, 1))),
    )

    for c in range(comps):

        @pl.when(has_left)
        def _():
            up_copy(c).wait_recv()

        @pl.when(has_right)
        def _():
            down_copy(c).wait_recv()

        if c < comps - 1:
            first, second = halo_mix(recv_ref, spread_ref, c, top)
            total_ref[:top] = (mix_ref[c, :top] + first).astype(BF16)
            total_ref[top:] = (mix_ref[c, top:] + second).astype(BF16)
        if c < comps - 2:
            out_ref[c] = out_ref[c] + dot_rows(both_ref[...], total_ref[...], half)

    @pl.when(has_right)
    def _():
        pltpu.make_async_remote_copy(
            src_ref=tail_ref, dst_ref=recv_ref.at[0], send_sem=send_sem.at[0], recv_sem=recv_sem.at[0, 0],
            device_id=(ves + 1, sec), device_id_type=MESH,
        ).wait_send()

    @pl.when(has_left)
    def _():
        pltpu.make_async_remote_copy(
            src_ref=head_ref, dst_ref=recv_ref.at[1], send_sem=send_sem.at[1], recv_sem=recv_sem.at[1, 0],
            device_id=(ves - 1, sec), device_id_type=MESH,
        ).wait_send()


def finish_kernel(
    part_ref,
    both_ref,
    mix_ref,
    total_ref,
    spread_ref,
    recv_ref,
    out_ref,
    result_ref,
    last_ref,
    done_sem,
    piece_sem,
):
    comps, num_points, _ = part_ref.shape
    last = comps - 1
    top = mix_ref.shape[1] - recv_ref.shape[2]
    half = num_points // 2
    stores = [
        pltpu.make_async_copy(part_ref.at[c], out_ref.at[c], done_sem.at[c])
        for c in range(comps - 2)
    ]
    for store in stores:
        store.start()
    first, second = halo_mix(recv_ref, spread_ref, last, top)
    last_ref[:top] = (mix_ref[last, :top] + first).astype(BF16)
    last_ref[top:] = (mix_ref[last, top:] + second).astype(BF16)
    for k, source in enumerate((total_ref, last_ref)):
        c = comps - 2 + k
        total = source[...]
        for i in range(2):
            rows = pl.ds(i * half, half)
            result_ref[k, rows] = part_ref[c, rows] + dot(both_ref[rows], total)
            store = pltpu.make_async_copy(
                result_ref.at[k, rows], out_ref.at[c, rows], piece_sem.at[k, i]
            )
            store.start()
            stores.append(store)
    for store in stores:
        store.wait()


def shards(
    n_ves,
    n_sec,
    density,
    analysis,
    synthesis,
    degree_gain,
    near_kernel,
    partners,
    pair_weight,
    wall_list,
    coupling,
    wall_gain,
):
    count, comps, num_points = density.shape
    num_coefs = analysis.shape[1]
    near_wall = wall_list.shape[0]
    panels, region_wall = coupling.shape
    tile = count // 2
    top = num_coefs // 2 // 16 * 16
    cut = num_coefs - top
    others = max(n_sec - 1, 1)
    vmem = pl.BlockSpec(memory_space=pltpu.VMEM)
    middle = pl.pallas_call(
        functools.partial(step_kernel, n_ves, n_sec),
        name="vesicle_step",
        out_shape=(
            jax.ShapeDtypeStruct((comps, num_points, count), F32),
            jax.ShapeDtypeStruct((num_points, num_coefs), BF16),
            jax.ShapeDtypeStruct((comps, num_coefs, count), F32),
            jax.ShapeDtypeStruct((num_coefs, count), BF16),
            jax.ShapeDtypeStruct((2, 2 * tile, count), BF16),
            jax.ShapeDtypeStruct((2, comps, cut, tile), BF16),
        ),
        in_specs=[pl.BlockSpec(memory_space=pltpu.HBM)] * 10,
        out_specs=[vmem] * 6,
        scratch_shapes=[
            pltpu.VMEM((comps, num_points, count), BF16),
            pltpu.VMEM((num_coefs, num_points), BF16),
            pltpu.VMEM((num_coefs, num_points), BF16),
            pltpu.VMEM((num_points, num_points), BF16),
            pltpu.VMEM(partners.shape[::-1], jnp.int32),
            pltpu.VMEM(partners.shape[::-1], F32),
            pltpu.SMEM((near_wall,), jnp.int32),
            pltpu.VMEM((region_wall, panels), BF16),
            pltpu.VMEM((1, panels), F32),
            pltpu.VMEM((num_coefs,), F32),
            pltpu.VMEM((num_points, num_coefs), BF16),
            pltpu.VMEM((comps, num_coefs, count), BF16),
            pltpu.VMEM((comps, cut, tile), BF16),
            pltpu.VMEM((comps, cut, tile), BF16),
            pltpu.VMEM((n_sec, comps, near_wall, num_coefs), BF16),
            pltpu.VMEM((others, region_wall, panels), BF16),
            pltpu.VMEM((others, 1, panels), F32),
            pltpu.SemaphoreType.DMA((2,)),
            pltpu.SemaphoreType.DMA((2, comps)),
            pltpu.SemaphoreType.DMA((3, others)),
        ],
        compiler_params=pltpu.CompilerParams(
            collective_id=0, has_side_effects=True, vmem_limit_bytes=32 * 1024 * 1024
        ),
    )(
        *(
            pltpu.with_memory_space_constraint(array, pltpu.HBM)
            for array in (
                density.transpose(1, 2, 0),
                analysis.T,
                synthesis,
                degree_gain,
                near_kernel,
                partners.T,
                pair_weight.T,
                wall_list,
                coupling.T,
                wall_gain.reshape(1, panels),
            )
        )
    )
    out = pl.pallas_call(
        finish_kernel,
        name="vesicle_finish",
        out_shape=jax.ShapeDtypeStruct((comps, num_points, count), F32),
        in_specs=[vmem] * 6,
        out_specs=pl.BlockSpec(memory_space=pltpu.HBM),
        scratch_shapes=[
            pltpu.VMEM((2, num_points, count), F32),
            pltpu.VMEM((num_coefs, count), BF16),
            pltpu.SemaphoreType.DMA((comps - 2,)),
            pltpu.SemaphoreType.DMA((2, 2)),
        ],
        compiler_params=pltpu.CompilerParams(vmem_limit_bytes=16 * 1024 * 1024),
    )(*middle)
    return out.transpose(2, 0, 1)


def solution(mesh):
    n_ves, n_sec = mesh.shape["ves"], mesh.shape["sec"]
    return jax.shard_map(
        functools.partial(shards, n_ves, n_sec),
        mesh=mesh,
        in_specs=(
            P(("ves", "sec"), None, None),
            P(),
            P(),
            P(),
            P(),
            P(("ves", "sec"), None),
            P(("ves", "sec"), None),
            P(("ves", "sec")),
            P(("ves", "sec"), None),
            P(("ves", "sec")),
        ),
        out_specs=P(("ves", "sec"), None, None),
        check_vma=False,
    )
```

```python
import functools

import jax
import jax.numpy as jnp
from jax import lax
from jax.experimental import pallas as pl
from jax.experimental.pallas import tpu as pltpu
from jax.sharding import PartitionSpec as P

MESH = pl.DeviceIdType.MESH
F32 = jnp.float32
BF16 = jnp.bfloat16

LATE_MIX = 1
LATE_OUT = 2
PIECES = 2


def dot(a, b, ca=1, cb=0):
    return lax.dot_general(a, b, (((ca,), (cb,)), ((), ())), preferred_element_type=F32)


def halo_mix(recv_ref, spread_ref, mix_ref, total_ref, c, top):
    halo = jnp.concatenate([recv_ref[0, c], recv_ref[1, c]], axis=1)
    total_ref[c, :top] = (mix_ref[c, :top] + dot(halo[:top], spread_ref[0])).astype(BF16)
    total_ref[c, top:] = (mix_ref[c, top:] + dot(halo, spread_ref[1])).astype(BF16)


def step_kernel(
    n_ves,
    n_sec,
    dens_in,
    ana_in,
    syn_in,
    gain_in,
    near_in,
    part_in,
    weight_in,
    list_in,
    coup_in,
    wgain_in,
    out_ref,
    both_ref,
    mix_ref,
    total_ref,
    spread_ref,
    recv_ref,
    dens_ref,
    ana_ref,
    syn_ref,
    near_ref,
    part_ref,
    weight_ref,
    list_ref,
    coup_ref,
    wgain_ref,
    gain_ref,
    syn_turned,
    coef_ref,
    edge_ref,
    pick_all,
    coup_all,
    gain_all,
    send_sem,
    recv_sem,
    wall_recv,
):
    ves = lax.axis_index("ves")
    sec = lax.axis_index("sec")
    comps, _, count = dens_ref.shape
    num_coefs = ana_ref.shape[0]
    near_wall = list_ref.shape[0]
    edge = count // 4
    tile = 2 * edge
    cut = recv_ref.shape[2]
    top = num_coefs - cut
    half = out_ref.shape[1] // 2
    has_left = ves > 0
    has_right = ves < n_ves - 1
    hops = range(1, n_sec)

    barrier = pltpu.get_barrier_semaphore()

    @pl.when(has_left)
    def _():
        pl.semaphore_signal(barrier, inc=1, device_id=(ves - 1, sec), device_id_type=MESH)

    @pl.when(has_right)
    def _():
        pl.semaphore_signal(barrier, inc=1, device_id=(ves + 1, sec), device_id_type=MESH)

    for hop in hops:
        peer = lax.rem(sec + hop, n_sec)
        pl.semaphore_signal(barrier, inc=1, device_id=(ves, peer), device_id_type=MESH)

    def halo_copy(side, part, to):
        return pltpu.make_async_remote_copy(
            src_ref=edge_ref.at[side, part],
            dst_ref=recv_ref.at[side, part],
            send_sem=send_sem.at[side],
            recv_sem=recv_sem.at[side, part],
            device_id=(to, sec),
            device_id_type=MESH,
        )

    def up_copy(c):
        return halo_copy(0, c, ves + 1)

    def down_copy(c):
        return halo_copy(1, c, ves - 1)

    turn = lax.rem(ves, 4)
    up_first = (turn == 0)
    greet_stage = jnp.where(ves == 0, jnp.where(sec == 0, 4, 2), jnp.where(turn == 0, 2, jnp.where(turn == 1, 0, jnp.where(turn == 2, 0, 0))))
    second_stage = jnp.where(ves == 0, 4, jnp.where(turn == 0, jnp.where(sec == 0, 3, 4), jnp.where(turn == 1, jnp.where(sec == 0, 3, 4), jnp.where(turn == 2, 3, 3))))

    def send(c, lead, when):
        up = up_first if lead else jnp.logical_not(up_first)

        @pl.when(when & has_right & up)
        def _():
            up_copy(c).start()

        @pl.when(when & has_left & jnp.logical_not(up))
        def _():
            down_copy(c).start()

    def at_stage(stage):
        @pl.when(greet_stage == stage)
        def _():
            sides = has_left.astype(jnp.int32) + has_right.astype(jnp.int32)
            pl.semaphore_wait(barrier, n_sec - 1 + sides)

        for c in range(comps):
            if c == stage:
                send(c, True, greet_stage <= stage)
            elif c < stage:
                send(c, True, greet_stage == stage)
        if stage >= comps:
            for c in range(comps):
                send(c, False, second_stage == stage)

    def work(load_sem, wall_send):
        pairs = [(ana_in, ana_ref)]
        pairs += [(dens_in.at[c], dens_ref.at[c]) for c in range(comps)]
        pairs += [
            (list_in, list_ref),
            (part_in, part_ref),
            (weight_in, weight_ref),
            (coup_in, coup_ref),
            (wgain_in, wgain_ref),
            (gain_in, gain_ref),
            (syn_in, syn_ref),
            (near_in, near_ref),
        ]
        loads = [
            pltpu.make_async_copy(src, dst, load_sem.at[i]) for i, (src, dst) in enumerate(pairs)
        ]
        for load in loads[:-2]:
            load.start()
        load_ana, *load_dens = loads[: comps + 1]
        load_list, load_part, load_weight, load_coup, load_wgain, load_gain, load_syn, load_near = (
            loads[comps + 1 :]
        )

        def wall_copy(hop, kind):
            src, dst = (
                (coup_in, coup_all.at[hop - 1]),
                (wgain_in, gain_all.at[hop - 1]),
                (pick_all.at[sec], pick_all.at[sec]),
            )[kind]
            return pltpu.make_async_remote_copy(
                src_ref=src,
                dst_ref=dst,
                send_sem=wall_send.at[kind, hop - 1],
                recv_sem=wall_recv.at[kind, hop - 1],
                device_id=(ves, lax.rem(sec + hop, n_sec)),
                device_id_type=MESH,
            )

        def send_walls(when):
            @pl.when(when)
            def _():
                for hop in hops:
                    for kind in (2, 0, 1):
                        wall_copy(hop, kind).start()

        @pl.when(jnp.logical_not(has_left))
        def _():
            recv_ref[0] = jnp.zeros(recv_ref.shape[1:], BF16)

        @pl.when(jnp.logical_not(has_right))
        def _():
            recv_ref[1] = jnp.zeros(recv_ref.shape[1:], BF16)

        low = lax.broadcasted_iota(jnp.int32, (cut, tile), 1) < edge
        load_ana.wait()

        def analyse(c, lanes):
            dens = dens_ref[c, :, lanes]
            return jnp.concatenate([dot(ana_ref[:top], dens), dot(ana_ref[top:], dens)], axis=0)

        def pack(part, upward):
            turned = pltpu.roll(part, edge, 1)
            tail = jnp.where(low, turned[:cut], part[top:])
            head = jnp.where(low, part[:cut], turned[top:])
            if upward is True or upward is False:
                return (tail if upward else head).astype(BF16)
            return jnp.where(upward, tail, head).astype(BF16)

        def analyse_side(upward):
            lanes = pl.ds(pl.multiple_of(jnp.where(upward, tile, 0), tile), tile)
            part = analyse(0, lanes)
            edge_ref[jnp.where(upward, 0, 1), 0] = pack(part, upward)
            return lanes, part

        load_dens[0].wait()
        lanes, part = analyse_side(up_first)
        at_stage(0)
        coef_ref[0, :, lanes] = part.astype(BF16)
        load_syn.start()
        load_near.start()
        for c in range(1, comps):
            load_dens[c].wait()
            full = analyse(c, slice(None))
            coef_ref[c] = full.astype(BF16)
            edge_ref[0, c] = pack(full[:, count - tile :], True)
            edge_ref[1, c] = pack(full[:, :tile], False)
            at_stage(c)
        lanes, part = analyse_side(jnp.logical_not(up_first))
        coef_ref[0, :, lanes] = part.astype(BF16)

        base = (ves * n_sec + sec) * count

        def placing(rows, first):
            row = lax.broadcasted_iota(jnp.int32, (rows, count), 0)
            ids = jnp.full((rows, count), -1, jnp.int32)
            for j in range(near_wall):
                ids = jnp.where(row == first + j, list_ref[j] - base, ids)
            hit = ids == lax.broadcasted_iota(jnp.int32, (rows, count), 1)
            return jnp.where(hit, 1.0, 0.0).astype(BF16)

        load_list.wait()
        choose = placing(near_wall, 0)
        for c in range(comps):
            pick_all[sec, c] = dot(choose, coef_ref[c], 1, 1).astype(BF16)
        at_stage(comps)
        send_walls(greet_stage <= comps)

        load_part.wait()
        load_weight.wait()
        shift = part_ref[...] - base
        weight = weight_ref[...]

        def mixing(rows, start):
            want = lax.broadcasted_iota(jnp.int32, (rows, count), 0) + start
            total = jnp.zeros((rows, count), F32)
            for k in range(shift.shape[0]):
                total = total + jnp.where(shift[k : k + 1, :] == want, weight[k : k + 1, :], 0.0)
            return total.astype(BF16)

        own_mix = mixing(count, 0)
        left_mix = mixing(edge, count - edge - n_sec * count)
        right_mix = mixing(edge, n_sec * count)
        none = jnp.zeros((edge, count), BF16)
        spread_ref[0] = jnp.concatenate([left_mix, none, right_mix, none], axis=0)
        spread_ref[1] = jnp.concatenate([none, left_mix, none, right_mix], axis=0)

        load_gain.wait()
        square = (num_coefs, num_coefs)
        diagonal = lax.broadcasted_iota(jnp.int32, square, 0) == lax.broadcasted_iota(
            jnp.int32, square, 1
        )
        gain = jnp.sum(
            jnp.where(diagonal, gain_ref[...].reshape(1, num_coefs), 0.0), axis=1, keepdims=True
        )

        for c in range(comps):
            mix_ref[c] = dot(coef_ref[c], own_mix)
        at_stage(comps + 1)
        send_walls(greet_stage > comps)

        load_syn.wait()
        syn_turned[...] = syn_ref[...].T
        load_near.wait()
        both_ref[...] = dot(near_ref[...].T, syn_turned[...]).astype(BF16)
        at_stage(comps + 2)

        for hop in hops:
            for kind in range(3):
                wall_copy(hop, kind).wait()
        load_coup.wait()
        load_wgain.wait()
        coup = jnp.concatenate([coup_ref[...]] + [coup_all[hop - 1] for hop in hops], axis=1)
        wgain = jnp.concatenate([wgain_ref[...]] + [gain_all[hop - 1] for hop in hops], axis=1)
        place = placing(near_wall * n_sec, sec * near_wall)
        for c in range(comps):
            picked = jnp.concatenate([pick_all[s, c] for s in range(n_sec)], axis=0)
            dens = (dot(picked, coup, 0, 0) * wgain).astype(BF16)
            back = dot(coup, dens, 1, 1).astype(BF16)
            wall = dot(back, place, 0, 0)
            scaled = coef_ref[c].astype(F32) * gain
            own = (scaled + wall).astype(BF16)
            out_ref[c, :half] = dot(syn_turned[:half], own)
            out_ref[c, half:] = dot(syn_turned[half:], own)

    pl.run_scoped(
        work,
        pltpu.SemaphoreType.DMA((comps + 9,)),
        pltpu.SemaphoreType.DMA((3, max(n_sec - 1, 1))),
    )

    for c in range(comps):

        @pl.when(has_left)
        def _():
            up_copy(c).wait_recv()

        @pl.when(has_right)
        def _():
            down_copy(c).wait_recv()

        if c < comps - LATE_MIX:
            halo_mix(recv_ref, spread_ref, mix_ref, total_ref, c, top)
        if c < comps - LATE_OUT:
            out_ref[c, :half] = out_ref[c, :half] + dot(both_ref[:half], total_ref[c])
            out_ref[c, half:] = out_ref[c, half:] + dot(both_ref[half:], total_ref[c])

    def sent(side, to):
        return pltpu.make_async_remote_copy(
            src_ref=edge_ref.at[side],
            dst_ref=recv_ref.at[side],
            send_sem=send_sem.at[side],
            recv_sem=recv_sem.at[side, 0],
            device_id=(to, sec),
            device_id_type=MESH,
        )

    @pl.when(has_right)
    def _():
        sent(0, ves + 1).wait_send()

    @pl.when(has_left)
    def _():
        sent(1, ves - 1).wait_send()


def finish_kernel(
    part_ref,
    both_ref,
    mix_ref,
    early_ref,
    spread_ref,
    recv_ref,
    out_ref,
    result_ref,
    total_ref,
    done_sem,
    piece_sem,
):
    comps, num_points, _ = part_ref.shape
    early = comps - LATE_OUT
    mixed = comps - LATE_MIX
    top = mix_ref.shape[1] - recv_ref.shape[2]
    rows = num_points // PIECES
    stores = [
        pltpu.make_async_copy(part_ref.at[c], out_ref.at[c], done_sem.at[c]) for c in range(early)
    ]
    for store in stores:
        store.start()
    for c in range(mixed, comps):
        halo_mix(recv_ref, spread_ref, mix_ref, total_ref, c, top)
    for c in range(early, comps):
        total = (early_ref if c < mixed else total_ref)[c]
        for i in range(PIECES):
            part = pl.ds(i * rows, rows)
            result_ref[c - early, part] = part_ref[c, part] + dot(both_ref[part], total)
            store = pltpu.make_async_copy(
                result_ref.at[c - early, part], out_ref.at[c, part], piece_sem.at[c - early, i]
            )
            store.start()
            stores.append(store)
    for store in stores:
        store.wait()


def shards(
    n_ves,
    n_sec,
    density,
    analysis,
    synthesis,
    degree_gain,
    near_kernel,
    partners,
    pair_weight,
    wall_list,
    coupling,
    wall_gain,
):
    count, comps, num_points = density.shape
    num_coefs = analysis.shape[1]
    near_wall = wall_list.shape[0]
    panels, region_wall = coupling.shape
    tile = count // 2
    top = num_coefs // 2 // 16 * 16
    cut = num_coefs - top
    others = max(n_sec - 1, 1)
    vmem = pl.BlockSpec(memory_space=pltpu.VMEM)
    middle = pl.pallas_call(
        functools.partial(step_kernel, n_ves, n_sec),
        name="vesicle_step",
        out_shape=(
            jax.ShapeDtypeStruct((comps, num_points, count), F32),
            jax.ShapeDtypeStruct((num_points, num_coefs), BF16),
            jax.ShapeDtypeStruct((comps, num_coefs, count), F32),
            jax.ShapeDtypeStruct((comps, num_coefs, count), BF16),
            jax.ShapeDtypeStruct((2, 2 * tile, count), BF16),
            jax.ShapeDtypeStruct((2, comps, cut, tile), BF16),
        ),
        in_specs=[pl.BlockSpec(memory_space=pltpu.HBM)] * 10,
        out_specs=[vmem] * 6,
        scratch_shapes=[
            pltpu.VMEM((comps, num_points, count), BF16),
            pltpu.VMEM((num_coefs, num_points), BF16),
            pltpu.VMEM((num_coefs, num_points), BF16),
            pltpu.VMEM((num_points, num_points), BF16),
            pltpu.VMEM(partners.shape[::-1], jnp.int32),
            pltpu.VMEM(partners.shape[::-1], F32),
            pltpu.SMEM((near_wall,), jnp.int32),
            pltpu.VMEM((region_wall, panels), BF16),
            pltpu.VMEM((1, panels), F32),
            pltpu.VMEM((num_coefs,), F32),
            pltpu.VMEM((num_points, num_coefs), BF16),
            pltpu.VMEM((comps, num_coefs, count), BF16),
            pltpu.VMEM((2, comps, cut, tile), BF16),
            pltpu.VMEM((n_sec, comps, near_wall, num_coefs), BF16),
            pltpu.VMEM((others, region_wall, panels), BF16),
            pltpu.VMEM((others, 1, panels), F32),
            pltpu.SemaphoreType.DMA((2,)),
            pltpu.SemaphoreType.DMA((2, comps)),
            pltpu.SemaphoreType.DMA((3, others)),
        ],
        compiler_params=pltpu.CompilerParams(
            collective_id=0, has_side_effects=True, vmem_limit_bytes=32 * 1024 * 1024
        ),
    )(
        *(
            pltpu.with_memory_space_constraint(array, pltpu.HBM)
            for array in (
                density.transpose(1, 2, 0),
                analysis.T,
                synthesis,
                degree_gain,
                near_kernel,
                partners.T,
                pair_weight.T,
                wall_list,
                coupling.T,
                wall_gain.reshape(1, panels),
            )
        )
    )
    out = pl.pallas_call(
        finish_kernel,
        name="vesicle_finish",
        out_shape=jax.ShapeDtypeStruct((comps, num_points, count), F32),
        in_specs=[vmem] * 6,
        out_specs=pl.BlockSpec(memory_space=pltpu.HBM),
        scratch_shapes=[
            pltpu.VMEM((LATE_OUT, num_points, count), F32),
            pltpu.VMEM((comps, num_coefs, count), BF16),
            pltpu.SemaphoreType.DMA((comps - LATE_OUT,)),
            pltpu.SemaphoreType.DMA((LATE_OUT, PIECES)),
        ],
        compiler_params=pltpu.CompilerParams(vmem_limit_bytes=16 * 1024 * 1024),
    )(*middle)
    return out.transpose(2, 0, 1)


def solution(mesh):
    n_ves, n_sec = mesh.shape["ves"], mesh.shape["sec"]
    return jax.shard_map(
        functools.partial(shards, n_ves, n_sec),
        mesh=mesh,
        in_specs=(
            P(("ves", "sec"), None, None),
            P(),
            P(),
            P(),
            P(),
            P(("ves", "sec"), None),
            P(("ves", "sec"), None),
            P(("ves", "sec")),
            P(("ves", "sec"), None),
            P(("ves", "sec")),
        ),
        out_specs=P(("ves", "sec"), None, None),
        check_vma=False,
    )
```

```python
import functools

import jax
import jax.numpy as jnp
from jax import lax
from jax.experimental import pallas as pl
from jax.experimental.pallas import tpu as pltpu
from jax.sharding import PartitionSpec as P

MESH = pl.DeviceIdType.MESH
F32 = jnp.float32
BF16 = jnp.bfloat16

LATE_MIX = 1
LATE_OUT = 2
PIECES = 4


def dot(a, b, ca=1, cb=0):
    return lax.dot_general(a, b, (((ca,), (cb,)), ((), ())), preferred_element_type=F32)


def halo_mix(recv_ref, spread_ref, mix_ref, total_ref, c, top):
    halo = jnp.concatenate([recv_ref[0, c], recv_ref[1, c]], axis=1)
    total_ref[c, :top] = (mix_ref[c, :top] + dot(halo[:top], spread_ref[0])).astype(BF16)
    total_ref[c, top:] = (mix_ref[c, top:] + dot(halo, spread_ref[1])).astype(BF16)


def step_kernel(
    n_ves,
    n_sec,
    dens_in,
    ana_in,
    syn_in,
    gain_in,
    near_in,
    part_in,
    weight_in,
    list_in,
    coup_in,
    wgain_in,
    out_ref,
    both_ref,
    mix_ref,
    total_ref,
    spread_ref,
    recv_ref,
    dens_ref,
    ana_ref,
    syn_ref,
    near_ref,
    part_ref,
    weight_ref,
    list_ref,
    coup_ref,
    wgain_ref,
    gain_ref,
    syn_turned,
    coef_ref,
    edge_ref,
    pick_all,
    coup_all,
    gain_all,
    send_sem,
    recv_sem,
    wall_recv,
):
    ves = lax.axis_index("ves")
    sec = lax.axis_index("sec")
    comps, _, count = dens_ref.shape
    num_coefs = ana_ref.shape[0]
    near_wall = list_ref.shape[0]
    edge = count // 4
    tile = 2 * edge
    cut = recv_ref.shape[2]
    top = num_coefs - cut
    half = out_ref.shape[1] // 2
    has_left = ves > 0
    has_right = ves < n_ves - 1
    hops = range(1, n_sec)

    barrier = pltpu.get_barrier_semaphore()

    def announce():
        @pl.when(has_left)
        def _():
            pl.semaphore_signal(barrier, inc=1, device_id=(ves - 1, sec), device_id_type=MESH)

        @pl.when(has_right)
        def _():
            pl.semaphore_signal(barrier, inc=1, device_id=(ves + 1, sec), device_id_type=MESH)

        for hop in hops:
            peer = lax.rem(sec + hop, n_sec)
            pl.semaphore_signal(barrier, inc=1, device_id=(ves, peer), device_id_type=MESH)

    def halo_copy(side, part, to):
        return pltpu.make_async_remote_copy(
            src_ref=edge_ref.at[side, part],
            dst_ref=recv_ref.at[side, part],
            send_sem=send_sem.at[0],
            recv_sem=recv_sem.at[part],
            device_id=(to, sec),
            device_id_type=MESH,
        )

    def up_copy(c):
        return halo_copy(0, c, ves + 1)

    def down_copy(c):
        return halo_copy(1, c, ves - 1)

    turn = lax.rem(ves, 4)
    up_first = (turn == 0)
    greet_stage = jnp.where(ves == 0, jnp.where(sec == 0, 4, 2), jnp.where(turn == 0, 2, jnp.where(turn == 1, 0, jnp.where(turn == 2, 0, 0))))
    second_stage = jnp.where(ves == 0, 4, jnp.where(turn == 0, jnp.where(sec == 0, 3, 4), jnp.where(turn == 1, jnp.where(sec == 0, 3, 4), jnp.where(turn == 2, 3, 3))))

    def send(c, lead, when):
        up = up_first if lead else jnp.logical_not(up_first)

        @pl.when(when & has_right & up)
        def _():
            up_copy(c).start()

        @pl.when(when & has_left & jnp.logical_not(up))
        def _():
            down_copy(c).start()

    def at_stage(stage):
        @pl.when(greet_stage == stage)
        def _():
            sides = has_left.astype(jnp.int32) + has_right.astype(jnp.int32)
            pl.semaphore_wait(barrier, n_sec - 1 + sides)

        for c in range(comps):
            if c == stage:
                send(c, True, greet_stage <= stage)
            elif c < stage:
                send(c, True, greet_stage == stage)
        if stage >= comps:
            for c in range(comps):
                send(c, False, second_stage == stage)

    def work(load_sem, wall_send):
        pairs = [(ana_in, ana_ref)]
        pairs += [(dens_in.at[c], dens_ref.at[c]) for c in range(comps)]
        pairs += [
            (list_in, list_ref),
            (part_in, part_ref),
            (weight_in, weight_ref),
            (coup_in, coup_ref),
            (wgain_in, wgain_ref),
            (gain_in, gain_ref),
            (syn_in, syn_ref),
            (near_in, near_ref),
        ]
        loads = [
            pltpu.make_async_copy(src, dst, load_sem.at[i]) for i, (src, dst) in enumerate(pairs)
        ]
        for load in loads[:2]:
            load.start()
        announce()
        for load in loads[2:-2]:
            load.start()
        load_ana, *load_dens = loads[: comps + 1]
        load_list, load_part, load_weight, load_coup, load_wgain, load_gain, load_syn, load_near = (
            loads[comps + 1 :]
        )

        def wall_copy(hop, kind):
            src, dst = (
                (coup_in, coup_all.at[hop - 1]),
                (wgain_in, gain_all.at[hop - 1]),
                (pick_all.at[sec], pick_all.at[sec]),
            )[kind]
            return pltpu.make_async_remote_copy(
                src_ref=src,
                dst_ref=dst,
                send_sem=wall_send.at[kind, hop - 1],
                recv_sem=wall_recv.at[kind, hop - 1],
                device_id=(ves, lax.rem(sec + hop, n_sec)),
                device_id_type=MESH,
            )

        def send_walls(when):
            @pl.when(when)
            def _():
                for hop in hops:
                    for kind in (2, 0, 1):
                        wall_copy(hop, kind).start()

        @pl.when(jnp.logical_not(has_left))
        def _():
            recv_ref[0] = jnp.zeros(recv_ref.shape[1:], BF16)

        @pl.when(jnp.logical_not(has_right))
        def _():
            recv_ref[1] = jnp.zeros(recv_ref.shape[1:], BF16)

        low = lax.broadcasted_iota(jnp.int32, (cut, tile), 1) < edge
        load_ana.wait()

        def analyse(c, lanes):
            dens = dens_ref[c, :, lanes]
            return jnp.concatenate([dot(ana_ref[:top], dens), dot(ana_ref[top:], dens)], axis=0)

        def pack(part, upward):
            turned = pltpu.roll(part, edge, 1)
            tail = jnp.where(low, turned[:cut], part[top:])
            head = jnp.where(low, part[:cut], turned[top:])
            if upward is True or upward is False:
                return (tail if upward else head).astype(BF16)
            return jnp.where(upward, tail, head).astype(BF16)

        def analyse_side(upward):
            lanes = pl.ds(pl.multiple_of(jnp.where(upward, tile, 0), tile), tile)
            part = analyse(0, lanes)
            edge_ref[jnp.where(upward, 0, 1), 0] = pack(part, upward)
            return lanes, part

        load_dens[0].wait()
        lanes, part = analyse_side(up_first)
        at_stage(0)
        coef_ref[0, :, lanes] = part.astype(BF16)
        load_syn.start()
        load_near.start()
        for c in range(1, comps):
            load_dens[c].wait()
            full = analyse(c, slice(None))
            coef_ref[c] = full.astype(BF16)
            edge_ref[0, c] = pack(full[:, count - tile :], True)
            edge_ref[1, c] = pack(full[:, :tile], False)
            at_stage(c)
        lanes, part = analyse_side(jnp.logical_not(up_first))
        coef_ref[0, :, lanes] = part.astype(BF16)

        base = (ves * n_sec + sec) * count

        def placing(rows, first):
            row = lax.broadcasted_iota(jnp.int32, (rows, count), 0)
            ids = jnp.full((rows, count), -1, jnp.int32)
            for j in range(near_wall):
                ids = jnp.where(row == first + j, list_ref[j] - base, ids)
            hit = ids == lax.broadcasted_iota(jnp.int32, (rows, count), 1)
            return jnp.where(hit, 1.0, 0.0).astype(BF16)

        load_list.wait()
        choose = placing(near_wall, 0)
        for c in range(comps):
            pick_all[sec, c] = dot(choose, coef_ref[c], 1, 1).astype(BF16)
        at_stage(comps)
        send_walls(greet_stage <= comps)

        load_part.wait()
        load_weight.wait()
        shift = part_ref[...] - base
        weight = weight_ref[...]

        def mixing(rows, start):
            want = lax.broadcasted_iota(jnp.int32, (rows, count), 0) + start
            total = jnp.zeros((rows, count), F32)
            for k in range(shift.shape[0]):
                total = total + jnp.where(shift[k : k + 1, :] == want, weight[k : k + 1, :], 0.0)
            return total.astype(BF16)

        own_mix = mixing(count, 0)
        left_mix = mixing(edge, count - edge - n_sec * count)
        right_mix = mixing(edge, n_sec * count)
        none = jnp.zeros((edge, count), BF16)
        spread_ref[0] = jnp.concatenate([left_mix, none, right_mix, none], axis=0)
        spread_ref[1] = jnp.concatenate([none, left_mix, none, right_mix], axis=0)

        load_gain.wait()
        square = (num_coefs, num_coefs)
        diagonal = lax.broadcasted_iota(jnp.int32, square, 0) == lax.broadcasted_iota(
            jnp.int32, square, 1
        )
        gain = jnp.sum(
            jnp.where(diagonal, gain_ref[...].reshape(1, num_coefs), 0.0), axis=1, keepdims=True
        )

        for c in range(comps):
            mix_ref[c] = dot(coef_ref[c], own_mix)
        at_stage(comps + 1)
        send_walls(greet_stage > comps)

        load_syn.wait()
        syn_turned[...] = syn_ref[...].T
        load_near.wait()
        both_ref[...] = dot(near_ref[...].T, syn_turned[...]).astype(BF16)
        at_stage(comps + 2)

        for hop in hops:
            for kind in range(3):
                wall_copy(hop, kind).wait()
        load_coup.wait()
        load_wgain.wait()
        coup = jnp.concatenate([coup_ref[...]] + [coup_all[hop - 1] for hop in hops], axis=1)
        wgain = jnp.concatenate([wgain_ref[...]] + [gain_all[hop - 1] for hop in hops], axis=1)
        place = placing(near_wall * n_sec, sec * near_wall)
        for c in range(comps):
            picked = jnp.concatenate([pick_all[s, c] for s in range(n_sec)], axis=0)
            dens = (dot(picked, coup, 0, 0) * wgain).astype(BF16)
            back = dot(coup, dens, 1, 1).astype(BF16)
            wall = dot(back, place, 0, 0)
            scaled = coef_ref[c].astype(F32) * gain
            own = (scaled + wall).astype(BF16)
            out_ref[c, :half] = dot(syn_turned[:half], own)
            out_ref[c, half:] = dot(syn_turned[half:], own)

    pl.run_scoped(
        work,
        pltpu.SemaphoreType.DMA((comps + 9,)),
        pltpu.SemaphoreType.DMA((3, max(n_sec - 1, 1))),
    )

    inner = has_left & has_right

    def pair(parts, c):
        return pltpu.make_async_remote_copy(
            src_ref=edge_ref.at[:, parts],
            dst_ref=recv_ref.at[:, parts],
            send_sem=send_sem.at[0],
            recv_sem=recv_sem.at[c],
            device_id=(ves, sec),
            device_id_type=MESH,
        )

    for c in range(comps):

        @pl.when(inner)
        def _():
            pair(pl.ds(c, 1), c).wait_recv()

        @pl.when(jnp.logical_not(inner))
        def _():
            up_copy(c).wait_recv()

        if c < comps - LATE_MIX:
            halo_mix(recv_ref, spread_ref, mix_ref, total_ref, c, top)
        if c < comps - LATE_OUT:
            out_ref[c, :half] = out_ref[c, :half] + dot(both_ref[:half], total_ref[c])
            out_ref[c, half:] = out_ref[c, half:] + dot(both_ref[half:], total_ref[c])

    @pl.when(inner)
    def _():
        pair(pl.ds(0, comps), 0).wait_send()

    @pl.when(jnp.logical_not(inner))
    def _():
        pltpu.make_async_remote_copy(
            src_ref=edge_ref.at[0],
            dst_ref=recv_ref.at[0],
            send_sem=send_sem.at[0],
            recv_sem=recv_sem.at[0],
            device_id=(ves, sec),
            device_id_type=MESH,
        ).wait_send()


def finish_kernel(
    part_ref,
    both_ref,
    mix_ref,
    early_ref,
    spread_ref,
    recv_ref,
    out_ref,
    result_ref,
    total_ref,
    done_sem,
    piece_sem,
):
    comps, num_points, _ = part_ref.shape
    early = comps - LATE_OUT
    mixed = comps - LATE_MIX
    top = mix_ref.shape[1] - recv_ref.shape[2]
    rows = num_points // PIECES
    stores = [
        pltpu.make_async_copy(part_ref.at[c], out_ref.at[c], done_sem.at[c]) for c in range(early)
    ]
    for store in stores:
        store.start()
    for c in range(mixed, comps):
        halo_mix(recv_ref, spread_ref, mix_ref, total_ref, c, top)
    for c in range(early, comps):
        total = (early_ref if c < mixed else total_ref)[c]
        for i in range(PIECES):
            part = pl.ds(i * rows, rows)
            result_ref[c - early, part] = part_ref[c, part] + dot(both_ref[part], total)
            store = pltpu.make_async_copy(
                result_ref.at[c - early, part], out_ref.at[c, part], piece_sem.at[c - early, i]
            )
            store.start()
            stores.append(store)
    for store in stores:
        store.wait()


def shards(
    n_ves,
    n_sec,
    density,
    analysis,
    synthesis,
    degree_gain,
    near_kernel,
    partners,
    pair_weight,
    wall_list,
    coupling,
    wall_gain,
):
    count, comps, num_points = density.shape
    num_coefs = analysis.shape[1]
    near_wall = wall_list.shape[0]
    panels, region_wall = coupling.shape
    tile = count // 2
    top = num_coefs // 2 // 16 * 16
    cut = num_coefs - top
    others = max(n_sec - 1, 1)
    vmem = pl.BlockSpec(memory_space=pltpu.VMEM)
    middle = pl.pallas_call(
        functools.partial(step_kernel, n_ves, n_sec),
        name="vesicle_step",
        out_shape=(
            jax.ShapeDtypeStruct((comps, num_points, count), F32),
            jax.ShapeDtypeStruct((num_points, num_coefs), BF16),
            jax.ShapeDtypeStruct((comps, num_coefs, count), F32),
            jax.ShapeDtypeStruct((comps, num_coefs, count), BF16),
            jax.ShapeDtypeStruct((2, 2 * tile, count), BF16),
            jax.ShapeDtypeStruct((2, comps, cut, tile), BF16),
        ),
        in_specs=[pl.BlockSpec(memory_space=pltpu.HBM)] * 10,
        out_specs=[vmem] * 6,
        scratch_shapes=[
            pltpu.VMEM((comps, num_points, count), BF16),
            pltpu.VMEM((num_coefs, num_points), BF16),
            pltpu.VMEM((num_coefs, num_points), BF16),
            pltpu.VMEM((num_points, num_points), BF16),
            pltpu.VMEM(partners.shape[::-1], jnp.int32),
            pltpu.VMEM(partners.shape[::-1], F32),
            pltpu.SMEM((near_wall,), jnp.int32),
            pltpu.VMEM((region_wall, panels), BF16),
            pltpu.VMEM((1, panels), F32),
            pltpu.VMEM((num_coefs,), F32),
            pltpu.VMEM((num_points, num_coefs), BF16),
            pltpu.VMEM((comps, num_coefs, count), BF16),
            pltpu.VMEM((2, comps, cut, tile), BF16),
            pltpu.VMEM((n_sec, comps, near_wall, num_coefs), BF16),
            pltpu.VMEM((others, region_wall, panels), BF16),
            pltpu.VMEM((others, 1, panels), F32),
            pltpu.SemaphoreType.DMA((1,)),
            pltpu.SemaphoreType.DMA((comps,)),
            pltpu.SemaphoreType.DMA((3, others)),
        ],
        compiler_params=pltpu.CompilerParams(
            collective_id=0, has_side_effects=True, vmem_limit_bytes=32 * 1024 * 1024
        ),
    )(
        *(
            pltpu.with_memory_space_constraint(array, pltpu.HBM)
            for array in (
                density.transpose(1, 2, 0),
                analysis.T,
                synthesis,
                degree_gain,
                near_kernel,
                partners.T,
                pair_weight.T,
                wall_list,
                coupling.T,
                wall_gain.reshape(1, panels),
            )
        )
    )
    out = pl.pallas_call(
        finish_kernel,
        name="vesicle_finish",
        out_shape=jax.ShapeDtypeStruct((comps, num_points, count), F32),
        in_specs=[vmem] * 6,
        out_specs=pl.BlockSpec(memory_space=pltpu.HBM),
        scratch_shapes=[
            pltpu.VMEM((LATE_OUT, num_points, count), F32),
            pltpu.VMEM((comps, num_coefs, count), BF16),
            pltpu.SemaphoreType.DMA((comps - LATE_OUT,)),
            pltpu.SemaphoreType.DMA((LATE_OUT, PIECES)),
        ],
        compiler_params=pltpu.CompilerParams(vmem_limit_bytes=16 * 1024 * 1024),
    )(*middle)
    return out.transpose(2, 0, 1)


def solution(mesh):
    n_ves, n_sec = mesh.shape["ves"], mesh.shape["sec"]
    return jax.shard_map(
        functools.partial(shards, n_ves, n_sec),
        mesh=mesh,
        in_specs=(
            P(("ves", "sec"), None, None),
            P(),
            P(),
            P(),
            P(),
            P(("ves", "sec"), None),
            P(("ves", "sec"), None),
            P(("ves", "sec")),
            P(("ves", "sec"), None),
            P(("ves", "sec")),
        ),
        out_specs=P(("ves", "sec"), None, None),
        check_vma=False,
    )
```

```python
import functools

import jax
import jax.numpy as jnp
from jax import lax
from jax.experimental import pallas as pl
from jax.experimental.pallas import tpu as pltpu
from jax.sharding import PartitionSpec as P

MESH = pl.DeviceIdType.MESH
F32 = jnp.float32
BF16 = jnp.bfloat16

LATE_MIX = 1
LATE_OUT = 2
PIECES = 4


def dot(a, b, ca=1, cb=0):
    return lax.dot_general(a, b, (((ca,), (cb,)), ((), ())), preferred_element_type=F32)


def halo_mix(recv_ref, spread_ref, mix_ref, total_ref, c, top):
    halo = jnp.concatenate([recv_ref[0, c], recv_ref[1, c]], axis=1)
    total_ref[c, :top] = (mix_ref[c, :top] + dot(halo[:top], spread_ref[0])).astype(BF16)
    total_ref[c, top:] = (mix_ref[c, top:] + dot(halo, spread_ref[1])).astype(BF16)


def step_kernel(
    n_ves,
    n_sec,
    dens_in,
    ana_in,
    syn_in,
    gain_in,
    near_in,
    part_in,
    weight_in,
    list_in,
    coup_in,
    wgain_in,
    out_ref,
    both_ref,
    mix_ref,
    total_ref,
    spread_ref,
    recv_ref,
    dens_ref,
    ana_ref,
    syn_ref,
    near_ref,
    part_ref,
    weight_ref,
    list_ref,
    coup_ref,
    wgain_ref,
    gain_ref,
    syn_turned,
    coef_ref,
    edge_ref,
    pick_all,
    coup_all,
    gain_all,
    send_sem,
    recv_sem,
    wall_recv,
):
    ves = lax.axis_index("ves")
    sec = lax.axis_index("sec")
    comps, _, count = dens_ref.shape
    num_coefs = ana_ref.shape[0]
    near_wall = list_ref.shape[0]
    edge = count // 4
    tile = 2 * edge
    cut = recv_ref.shape[2]
    top = num_coefs - cut
    half = out_ref.shape[1] // 2
    has_left = ves > 0
    has_right = ves < n_ves - 1
    hops = range(1, n_sec)

    barrier = pltpu.get_barrier_semaphore()

    def announce():
        @pl.when(has_left)
        def _():
            pl.semaphore_signal(barrier, inc=1, device_id=(ves - 1, sec), device_id_type=MESH)

        @pl.when(has_right)
        def _():
            pl.semaphore_signal(barrier, inc=1, device_id=(ves + 1, sec), device_id_type=MESH)

        for hop in hops:
            peer = lax.rem(sec + hop, n_sec)
            pl.semaphore_signal(barrier, inc=1, device_id=(ves, peer), device_id_type=MESH)

    def halo_copy(side, part, to):
        return pltpu.make_async_remote_copy(
            src_ref=edge_ref.at[side, part],
            dst_ref=recv_ref.at[side, part],
            send_sem=send_sem.at[0],
            recv_sem=recv_sem.at[part],
            device_id=(to, sec),
            device_id_type=MESH,
        )

    def up_copy(c):
        return halo_copy(0, c, ves + 1)

    def down_copy(c):
        return halo_copy(1, c, ves - 1)

    turn = lax.rem(ves, 4)
    up_first = (turn == 0)
    greet_stage = jnp.where(ves == 0, jnp.where(sec == 0, 4, 2), jnp.where(turn == 0, 2, jnp.where(turn == 1, 0, jnp.where(turn == 2, 0, 0))))
    second_stage = jnp.where(ves == 0, 4, jnp.where(turn == 0, jnp.where(sec == 0, 3, 4), jnp.where(turn == 1, jnp.where(sec == 0, 3, 4), jnp.where(turn == 2, 3, 3))))

    def send(c, lead, when):
        up = up_first if lead else jnp.logical_not(up_first)

        @pl.when(when & has_right & up)
        def _():
            up_copy(c).start()

        @pl.when(when & has_left & jnp.logical_not(up))
        def _():
            down_copy(c).start()

    def at_stage(stage):
        @pl.when(greet_stage == stage)
        def _():
            sides = has_left.astype(jnp.int32) + has_right.astype(jnp.int32)
            pl.semaphore_wait(barrier, n_sec - 1 + sides)

        for c in range(comps):
            if c == stage:
                send(c, True, greet_stage <= stage)
            elif c < stage:
                send(c, True, greet_stage == stage)
        if stage >= comps:
            for c in range(comps):
                send(c, False, second_stage == stage)

    def work(load_sem, wall_send):
        pairs = [(ana_in, ana_ref)]
        pairs += [(dens_in.at[c], dens_ref.at[c]) for c in range(comps)]
        pairs += [
            (list_in, list_ref),
            (part_in, part_ref),
            (weight_in, weight_ref),
            (coup_in, coup_ref),
            (wgain_in, wgain_ref),
            (gain_in, gain_ref),
            (syn_in, syn_ref),
            (near_in, near_ref),
        ]
        loads = [
            pltpu.make_async_copy(src, dst, load_sem.at[i]) for i, (src, dst) in enumerate(pairs)
        ]
        for load in loads[:2]:
            load.start()
        announce()
        for load in loads[2:-2]:
            load.start()
        load_ana, *load_dens = loads[: comps + 1]
        load_list, load_part, load_weight, load_coup, load_wgain, load_gain, load_syn, load_near = (
            loads[comps + 1 :]
        )

        def wall_copy(hop, kind):
            src, dst = (
                (coup_in, coup_all.at[hop - 1]),
                (wgain_in, gain_all.at[hop - 1]),
                (pick_all.at[sec], pick_all.at[sec]),
            )[kind]
            return pltpu.make_async_remote_copy(
                src_ref=src,
                dst_ref=dst,
                send_sem=wall_send.at[kind, hop - 1],
                recv_sem=wall_recv.at[kind, hop - 1],
                device_id=(ves, lax.rem(sec + hop, n_sec)),
                device_id_type=MESH,
            )

        def send_walls(when):
            @pl.when(when)
            def _():
                for hop in hops:
                    for kind in (2, 0, 1):
                        wall_copy(hop, kind).start()

        @pl.when(jnp.logical_not(has_left))
        def _():
            recv_ref[0] = jnp.zeros(recv_ref.shape[1:], BF16)

        @pl.when(jnp.logical_not(has_right))
        def _():
            recv_ref[1] = jnp.zeros(recv_ref.shape[1:], BF16)

        low = lax.broadcasted_iota(jnp.int32, (cut, tile), 1) < edge
        load_ana.wait()

        def analyse(c, lanes):
            dens = dens_ref[c, :, lanes]
            return jnp.concatenate([dot(ana_ref[:top], dens), dot(ana_ref[top:], dens)], axis=0)

        def pack(part, upward):
            turned = pltpu.roll(part, edge, 1)
            tail = jnp.where(low, turned[:cut], part[top:])
            head = jnp.where(low, part[:cut], turned[top:])
            if upward is True or upward is False:
                return (tail if upward else head).astype(BF16)
            return jnp.where(upward, tail, head).astype(BF16)

        def analyse_side(upward):
            lanes = pl.ds(pl.multiple_of(jnp.where(upward, tile, 0), tile), tile)
            part = analyse(0, lanes)
            edge_ref[jnp.where(upward, 0, 1), 0] = pack(part, upward)
            return lanes, part

        load_dens[0].wait()
        lanes, part = analyse_side(up_first)
        at_stage(0)
        coef_ref[0, :, lanes] = part.astype(BF16)
        load_syn.start()
        load_near.start()
        for c in range(1, comps):
            load_dens[c].wait()
            full = analyse(c, slice(None))
            coef_ref[c] = full.astype(BF16)
            edge_ref[0, c] = pack(full[:, count - tile :], True)
            edge_ref[1, c] = pack(full[:, :tile], False)
            at_stage(c)
        lanes, part = analyse_side(jnp.logical_not(up_first))
        coef_ref[0, :, lanes] = part.astype(BF16)

        base = (ves * n_sec + sec) * count

        def placing(rows, first):
            row = lax.broadcasted_iota(jnp.int32, (rows, count), 0)
            ids = jnp.full((rows, count), -1, jnp.int32)
            for j in range(near_wall):
                ids = jnp.where(row == first + j, list_ref[j] - base, ids)
            hit = ids == lax.broadcasted_iota(jnp.int32, (rows, count), 1)
            return jnp.where(hit, 1.0, 0.0).astype(BF16)

        load_list.wait()
        choose = placing(near_wall, 0)
        for c in range(comps):
            pick_all[sec, c] = dot(choose, coef_ref[c], 1, 1).astype(BF16)
        at_stage(comps)
        send_walls(greet_stage <= comps)

        load_part.wait()
        load_weight.wait()
        shift = part_ref[...] - base
        weight = weight_ref[...]

        def mixing(rows, start):
            want = lax.broadcasted_iota(jnp.int32, (rows, count), 0) + start
            total = jnp.zeros((rows, count), F32)
            for k in range(shift.shape[0]):
                total = total + jnp.where(shift[k : k + 1, :] == want, weight[k : k + 1, :], 0.0)
            return total.astype(BF16)

        own_mix = mixing(count, 0)
        left_mix = mixing(edge, count - edge - n_sec * count)
        right_mix = mixing(edge, n_sec * count)
        none = jnp.zeros((edge, count), BF16)
        spread_ref[0] = jnp.concatenate([left_mix, none, right_mix, none], axis=0)
        spread_ref[1] = jnp.concatenate([none, left_mix, none, right_mix], axis=0)

        load_gain.wait()
        square = (num_coefs, num_coefs)
        diagonal = lax.broadcasted_iota(jnp.int32, square, 0) == lax.broadcasted_iota(
            jnp.int32, square, 1
        )
        gain = jnp.sum(
            jnp.where(diagonal, gain_ref[...].reshape(1, num_coefs), 0.0), axis=1, keepdims=True
        )

        for c in range(comps):
            mix_ref[c] = dot(coef_ref[c], own_mix)
        at_stage(comps + 1)
        send_walls(greet_stage > comps)

        load_syn.wait()
        syn_turned[...] = syn_ref[...].T
        load_near.wait()
        both_ref[...] = dot(near_ref[...].T, syn_turned[...]).astype(BF16)
        at_stage(comps + 2)

        for hop in hops:
            for kind in range(3):
                wall_copy(hop, kind).wait()
        load_coup.wait()
        load_wgain.wait()
        coup = jnp.concatenate([coup_ref[...]] + [coup_all[hop - 1] for hop in hops], axis=1)
        wgain = jnp.concatenate([wgain_ref[...]] + [gain_all[hop - 1] for hop in hops], axis=1)
        place = placing(near_wall * n_sec, sec * near_wall)
        for c in range(comps):
            picked = jnp.concatenate([pick_all[s, c] for s in range(n_sec)], axis=0)
            dens = (dot(picked, coup, 0, 0) * wgain).astype(BF16)
            back = dot(coup, dens, 1, 1).astype(BF16)
            wall = dot(back, place, 0, 0)
            scaled = coef_ref[c].astype(F32) * gain
            own = (scaled + wall).astype(BF16)
            out_ref[c, :half] = dot(syn_turned[:half], own)
            out_ref[c, half:] = dot(syn_turned[half:], own)

    pl.run_scoped(
        work,
        pltpu.SemaphoreType.DMA((comps + 9,)),
        pltpu.SemaphoreType.DMA((3, max(n_sec - 1, 1))),
    )

    inner = has_left & has_right

    def pair(parts, c):
        return pltpu.make_async_remote_copy(
            src_ref=edge_ref.at[:, parts],
            dst_ref=recv_ref.at[:, parts],
            send_sem=send_sem.at[0],
            recv_sem=recv_sem.at[c],
            device_id=(ves, sec),
            device_id_type=MESH,
        )

    for c in range(comps):

        @pl.when(inner)
        def _():
            pair(pl.ds(c, 1), c).wait_recv()

        @pl.when(jnp.logical_not(inner))
        def _():
            up_copy(c).wait_recv()

        if c < comps - LATE_MIX:
            halo_mix(recv_ref, spread_ref, mix_ref, total_ref, c, top)
        if c < comps - LATE_OUT:
            out_ref[c, :half] = out_ref[c, :half] + dot(both_ref[:half], total_ref[c])
            out_ref[c, half:] = out_ref[c, half:] + dot(both_ref[half:], total_ref[c])

    @pl.when(inner)
    def _():
        pair(pl.ds(0, comps), 0).wait_send()

    @pl.when(jnp.logical_not(inner))
    def _():
        pltpu.make_async_remote_copy(
            src_ref=edge_ref.at[0],
            dst_ref=recv_ref.at[0],
            send_sem=send_sem.at[0],
            recv_sem=recv_sem.at[0],
            device_id=(ves, sec),
            device_id_type=MESH,
        ).wait_send()


def finish_kernel(
    part_ref,
    both_ref,
    mix_ref,
    early_ref,
    spread_ref,
    recv_ref,
    out_ref,
    result_ref,
    done_sem,
    piece_sem,
):
    comps, num_points, _ = part_ref.shape
    early = comps - LATE_OUT
    mixed = comps - LATE_MIX
    top = mix_ref.shape[1] - recv_ref.shape[2]
    rows = num_points // PIECES
    stores = [
        pltpu.make_async_copy(part_ref.at[c], out_ref.at[c], done_sem.at[c]) for c in range(early)
    ]
    for store in stores:
        store.start()
    late = []
    for c in range(mixed, comps):
        halo = jnp.concatenate([recv_ref[0, c], recv_ref[1, c]], axis=1)
        upper = (mix_ref[c, :top] + dot(halo[:top], spread_ref[0])).astype(BF16)
        lower = (mix_ref[c, top:] + dot(halo, spread_ref[1])).astype(BF16)
        late.append(jnp.concatenate([upper, lower], axis=0))
    for c in range(early, comps):
        total = early_ref[c] if c < mixed else late[c - mixed]
        for i in range(PIECES):
            part = pl.ds(i * rows, rows)
            result_ref[c - early, part] = part_ref[c, part] + dot(both_ref[part], total)
            store = pltpu.make_async_copy(
                result_ref.at[c - early, part], out_ref.at[c, part], piece_sem.at[c - early, i]
            )
            store.start()
            stores.append(store)
    for store in stores:
        store.wait()


def shards(
    n_ves,
    n_sec,
    density,
    analysis,
    synthesis,
    degree_gain,
    near_kernel,
    partners,
    pair_weight,
    wall_list,
    coupling,
    wall_gain,
):
    count, comps, num_points = density.shape
    num_coefs = analysis.shape[1]
    near_wall = wall_list.shape[0]
    panels, region_wall = coupling.shape
    tile = count // 2
    top = num_coefs // 2 // 16 * 16
    cut = num_coefs - top
    others = max(n_sec - 1, 1)
    vmem = pl.BlockSpec(memory_space=pltpu.VMEM)
    middle = pl.pallas_call(
        functools.partial(step_kernel, n_ves, n_sec),
        name="vesicle_step",
        out_shape=(
            jax.ShapeDtypeStruct((comps, num_points, count), F32),
            jax.ShapeDtypeStruct((num_points, num_coefs), BF16),
            jax.ShapeDtypeStruct((comps, num_coefs, count), F32),
            jax.ShapeDtypeStruct((comps, num_coefs, count), BF16),
            jax.ShapeDtypeStruct((2, 2 * tile, count), BF16),
            jax.ShapeDtypeStruct((2, comps, cut, tile), BF16),
        ),
        in_specs=[pl.BlockSpec(memory_space=pltpu.HBM)] * 10,
        out_specs=[vmem] * 6,
        scratch_shapes=[
            pltpu.VMEM((comps, num_points, count), BF16),
            pltpu.VMEM((num_coefs, num_points), BF16),
            pltpu.VMEM((num_coefs, num_points), BF16),
            pltpu.VMEM((num_points, num_points), BF16),
            pltpu.VMEM(partners.shape[::-1], jnp.int32),
            pltpu.VMEM(partners.shape[::-1], F32),
            pltpu.SMEM((near_wall,), jnp.int32),
            pltpu.VMEM((region_wall, panels), BF16),
            pltpu.VMEM((1, panels), F32),
            pltpu.VMEM((num_coefs,), F32),
            pltpu.VMEM((num_points, num_coefs), BF16),
            pltpu.VMEM((comps, num_coefs, count), BF16),
            pltpu.VMEM((2, comps, cut, tile), BF16),
            pltpu.VMEM((n_sec, comps, near_wall, num_coefs), BF16),
            pltpu.VMEM((others, region_wall, panels), BF16),
            pltpu.VMEM((others, 1, panels), F32),
            pltpu.SemaphoreType.DMA((1,)),
            pltpu.SemaphoreType.DMA((comps,)),
            pltpu.SemaphoreType.DMA((3, others)),
        ],
        compiler_params=pltpu.CompilerParams(
            collective_id=0, has_side_effects=True, vmem_limit_bytes=32 * 1024 * 1024
        ),
    )(
        *(
            pltpu.with_memory_space_constraint(array, pltpu.HBM)
            for array in (
                density.transpose(1, 2, 0),
                analysis.T,
                synthesis,
                degree_gain,
                near_kernel,
                partners.T,
                pair_weight.T,
                wall_list,
                coupling.T,
                wall_gain.reshape(1, panels),
            )
        )
    )
    out = pl.pallas_call(
        finish_kernel,
        name="vesicle_finish",
        out_shape=jax.ShapeDtypeStruct((comps, num_points, count), F32),
        in_specs=[vmem] * 6,
        out_specs=pl.BlockSpec(memory_space=pltpu.HBM),
        scratch_shapes=[
            pltpu.VMEM((LATE_OUT, num_points, count), F32),
            pltpu.SemaphoreType.DMA((comps - LATE_OUT,)),
            pltpu.SemaphoreType.DMA((LATE_OUT, PIECES)),
        ],
        compiler_params=pltpu.CompilerParams(vmem_limit_bytes=16 * 1024 * 1024),
    )(*middle)
    return out.transpose(2, 0, 1)


def solution(mesh):
    n_ves, n_sec = mesh.shape["ves"], mesh.shape["sec"]
    return jax.shard_map(
        functools.partial(shards, n_ves, n_sec),
        mesh=mesh,
        in_specs=(
            P(("ves", "sec"), None, None),
            P(),
            P(),
            P(),
            P(),
            P(("ves", "sec"), None),
            P(("ves", "sec"), None),
            P(("ves", "sec")),
            P(("ves", "sec"), None),
            P(("ves", "sec")),
        ),
        out_specs=P(("ves", "sec"), None, None),
        check_vma=False,
    )
```

```python
import functools

import jax
import jax.numpy as jnp
from jax import lax
from jax.experimental import pallas as pl
from jax.experimental.pallas import tpu as pltpu
from jax.sharding import PartitionSpec as P

MESH = pl.DeviceIdType.MESH
F32 = jnp.float32
BF16 = jnp.bfloat16

LATE_MIX = 1
LATE_OUT = 2
PIECES = 4


def dot(a, b, ca=1, cb=0):
    return lax.dot_general(a, b, (((ca,), (cb,)), ((), ())), preferred_element_type=F32)


def halo_mix(recv_ref, spread_ref, mix_ref, total_ref, c, top):
    halo = jnp.concatenate([recv_ref[0, c], recv_ref[1, c]], axis=1)
    total_ref[c, :top] = (mix_ref[c, :top] + dot(halo[:top], spread_ref[0])).astype(BF16)
    total_ref[c, top:] = (mix_ref[c, top:] + dot(halo, spread_ref[1])).astype(BF16)


def step_kernel(
    n_ves,
    n_sec,
    dens_in,
    ana_in,
    syn_in,
    gain_in,
    near_in,
    part_in,
    weight_in,
    list_in,
    coup_in,
    wgain_in,
    out_ref,
    both_ref,
    mix_ref,
    total_ref,
    spread_ref,
    recv_ref,
    dens_ref,
    ana_ref,
    syn_ref,
    near_ref,
    part_ref,
    weight_ref,
    list_ref,
    coup_ref,
    wgain_ref,
    gain_ref,
    syn_turned,
    coef_ref,
    edge_ref,
    pick_all,
    coup_all,
    gain_all,
    send_sem,
    recv_sem,
    wall_recv,
):
    ves = lax.axis_index("ves")
    sec = lax.axis_index("sec")
    comps, _, count = dens_ref.shape
    num_coefs = ana_ref.shape[0]
    near_wall = list_ref.shape[0]
    edge = count // 4
    tile = 2 * edge
    cut = recv_ref.shape[2]
    top = num_coefs - cut
    half = out_ref.shape[1] // 2
    has_left = ves > 0
    has_right = ves < n_ves - 1
    hops = range(1, n_sec)

    barrier = pltpu.get_barrier_semaphore()

    def announce():
        @pl.when(has_left)
        def _():
            pl.semaphore_signal(barrier, inc=1, device_id=(ves - 1, sec), device_id_type=MESH)

        @pl.when(has_right)
        def _():
            pl.semaphore_signal(barrier, inc=1, device_id=(ves + 1, sec), device_id_type=MESH)

        for hop in hops:
            peer = lax.rem(sec + hop, n_sec)
            pl.semaphore_signal(barrier, inc=1, device_id=(ves, peer), device_id_type=MESH)

    def halo_copy(side, part, to):
        return pltpu.make_async_remote_copy(
            src_ref=edge_ref.at[side, part],
            dst_ref=recv_ref.at[side, part],
            send_sem=send_sem.at[0],
            recv_sem=recv_sem.at[part],
            device_id=(to, sec),
            device_id_type=MESH,
        )

    def up_copy(c):
        return halo_copy(0, c, ves + 1)

    def down_copy(c):
        return halo_copy(1, c, ves - 1)

    turn = lax.rem(ves, 4)
    up_first = (turn == 0)
    greet_stage = jnp.where(ves == 0, jnp.where(sec == 0, 4, 2), jnp.where(turn == 0, 2, jnp.where(turn == 1, 0, jnp.where(turn == 2, 0, 0))))
    second_stage = jnp.where(ves == 0, 4, jnp.where(turn == 0, jnp.where(sec == 0, 3, 4), jnp.where(turn == 1, jnp.where(sec == 0, 3, 4), jnp.where(turn == 2, 3, 3))))

    def send(c, lead, when):
        up = up_first if lead else jnp.logical_not(up_first)

        @pl.when(when & has_right & up)
        def _():
            up_copy(c).start()

        @pl.when(when & has_left & jnp.logical_not(up))
        def _():
            down_copy(c).start()

    def at_stage(stage):
        @pl.when(greet_stage == stage)
        def _():
            sides = has_left.astype(jnp.int32) + has_right.astype(jnp.int32)
            pl.semaphore_wait(barrier, n_sec - 1 + sides)

        for c in range(comps):
            if c == stage:
                send(c, True, greet_stage <= stage)
            elif c < stage:
                send(c, True, greet_stage == stage)
        if stage >= comps:
            for c in range(comps):
                spread = (turn == 3) & (sec == 1) if c == comps - 1 else False
                send(c, False, jnp.where(spread, 4, second_stage) == stage)

    def work(load_sem, wall_send):
        pairs = [(ana_in, ana_ref)]
        pairs += [(dens_in.at[c], dens_ref.at[c]) for c in range(comps)]
        pairs += [
            (list_in, list_ref),
            (part_in, part_ref),
            (weight_in, weight_ref),
            (coup_in, coup_ref),
            (wgain_in, wgain_ref),
            (gain_in, gain_ref),
            (syn_in, syn_ref),
            (near_in, near_ref),
        ]
        loads = [
            pltpu.make_async_copy(src, dst, load_sem.at[i]) for i, (src, dst) in enumerate(pairs)
        ]
        for load in loads[:2]:
            load.start()
        announce()
        for load in loads[2:-2]:
            load.start()
        load_ana, *load_dens = loads[: comps + 1]
        load_list, load_part, load_weight, load_coup, load_wgain, load_gain, load_syn, load_near = (
            loads[comps + 1 :]
        )

        def wall_copy(hop, kind):
            src, dst = (
                (coup_in, coup_all.at[hop - 1]),
                (wgain_in, gain_all.at[hop - 1]),
                (pick_all.at[sec], pick_all.at[sec]),
            )[kind]
            return pltpu.make_async_remote_copy(
                src_ref=src,
                dst_ref=dst,
                send_sem=wall_send.at[kind, hop - 1],
                recv_sem=wall_recv.at[kind, hop - 1],
                device_id=(ves, lax.rem(sec + hop, n_sec)),
                device_id_type=MESH,
            )

        def send_walls(when):
            @pl.when(when)
            def _():
                for hop in hops:
                    for kind in (2, 0, 1):
                        wall_copy(hop, kind).start()

        @pl.when(jnp.logical_not(has_left))
        def _():
            recv_ref[0] = jnp.zeros(recv_ref.shape[1:], BF16)

        @pl.when(jnp.logical_not(has_right))
        def _():
            recv_ref[1] = jnp.zeros(recv_ref.shape[1:], BF16)

        low = lax.broadcasted_iota(jnp.int32, (cut, tile), 1) < edge
        load_ana.wait()

        def analyse(c, lanes):
            dens = dens_ref[c, :, lanes]
            return jnp.concatenate([dot(ana_ref[:top], dens), dot(ana_ref[top:], dens)], axis=0)

        def pack(part, upward):
            turned = pltpu.roll(part, edge, 1)
            tail = jnp.where(low, turned[:cut], part[top:])
            head = jnp.where(low, part[:cut], turned[top:])
            if upward is True or upward is False:
                return (tail if upward else head).astype(BF16)
            return jnp.where(upward, tail, head).astype(BF16)

        def analyse_side(upward):
            lanes = pl.ds(pl.multiple_of(jnp.where(upward, tile, 0), tile), tile)
            part = analyse(0, lanes)
            edge_ref[jnp.where(upward, 0, 1), 0] = pack(part, upward)
            return lanes, part

        load_dens[0].wait()
        lanes, part = analyse_side(up_first)
        at_stage(0)
        coef_ref[0, :, lanes] = part.astype(BF16)
        load_syn.start()
        load_near.start()
        for c in range(1, comps):
            load_dens[c].wait()
            full = analyse(c, slice(None))
            coef_ref[c] = full.astype(BF16)
            edge_ref[0, c] = pack(full[:, count - tile :], True)
            edge_ref[1, c] = pack(full[:, :tile], False)
            at_stage(c)
        lanes, part = analyse_side(jnp.logical_not(up_first))
        coef_ref[0, :, lanes] = part.astype(BF16)

        base = (ves * n_sec + sec) * count

        def placing(rows, first):
            row = lax.broadcasted_iota(jnp.int32, (rows, count), 0)
            ids = jnp.full((rows, count), -1, jnp.int32)
            for j in range(near_wall):
                ids = jnp.where(row == first + j, list_ref[j] - base, ids)
            hit = ids == lax.broadcasted_iota(jnp.int32, (rows, count), 1)
            return jnp.where(hit, 1.0, 0.0).astype(BF16)

        load_list.wait()
        choose = placing(near_wall, 0)
        for c in range(comps):
            pick_all[sec, c] = dot(choose, coef_ref[c], 1, 1).astype(BF16)
        at_stage(comps)
        send_walls(greet_stage <= comps)

        load_part.wait()
        load_weight.wait()
        shift = part_ref[...] - base
        weight = weight_ref[...]

        def mixing(rows, start):
            want = lax.broadcasted_iota(jnp.int32, (rows, count), 0) + start
            total = jnp.zeros((rows, count), F32)
            for k in range(shift.shape[0]):
                total = total + jnp.where(shift[k : k + 1, :] == want, weight[k : k + 1, :], 0.0)
            return total.astype(BF16)

        own_mix = mixing(count, 0)
        left_mix = mixing(edge, count - edge - n_sec * count)
        right_mix = mixing(edge, n_sec * count)
        none = jnp.zeros((edge, count), BF16)
        spread_ref[0] = jnp.concatenate([left_mix, none, right_mix, none], axis=0)
        spread_ref[1] = jnp.concatenate([none, left_mix, none, right_mix], axis=0)

        load_gain.wait()
        square = (num_coefs, num_coefs)
        diagonal = lax.broadcasted_iota(jnp.int32, square, 0) == lax.broadcasted_iota(
            jnp.int32, square, 1
        )
        gain = jnp.sum(
            jnp.where(diagonal, gain_ref[...].reshape(1, num_coefs), 0.0), axis=1, keepdims=True
        )

        for c in range(comps):
            mix_ref[c] = dot(coef_ref[c], own_mix)
        at_stage(comps + 1)
        send_walls(greet_stage > comps)

        load_syn.wait()
        syn_turned[...] = syn_ref[...].T
        load_near.wait()
        both_ref[...] = dot(near_ref[...].T, syn_turned[...]).astype(BF16)
        at_stage(comps + 2)

        for hop in hops:
            for kind in range(3):
                wall_copy(hop, kind).wait()
        load_coup.wait()
        load_wgain.wait()
        coup = jnp.concatenate([coup_ref[...]] + [coup_all[hop - 1] for hop in hops], axis=1)
        wgain = jnp.concatenate([wgain_ref[...]] + [gain_all[hop - 1] for hop in hops], axis=1)
        place = placing(near_wall * n_sec, sec * near_wall)
        for c in range(comps):
            picked = jnp.concatenate([pick_all[s, c] for s in range(n_sec)], axis=0)
            dens = (dot(picked, coup, 0, 0) * wgain).astype(BF16)
            back = dot(coup, dens, 1, 1).astype(BF16)
            wall = dot(back, place, 0, 0)
            scaled = coef_ref[c].astype(F32) * gain
            own = (scaled + wall).astype(BF16)
            out_ref[c, :half] = dot(syn_turned[:half], own)
            out_ref[c, half:] = dot(syn_turned[half:], own)

    pl.run_scoped(
        work,
        pltpu.SemaphoreType.DMA((comps + 9,)),
        pltpu.SemaphoreType.DMA((3, max(n_sec - 1, 1))),
    )

    inner = has_left & has_right

    def pair(parts, c):
        return pltpu.make_async_remote_copy(
            src_ref=edge_ref.at[:, parts],
            dst_ref=recv_ref.at[:, parts],
            send_sem=send_sem.at[0],
            recv_sem=recv_sem.at[c],
            device_id=(ves, sec),
            device_id_type=MESH,
        )

    for c in range(comps):

        @pl.when(inner)
        def _():
            pair(pl.ds(c, 1), c).wait_recv()

        @pl.when(jnp.logical_not(inner))
        def _():
            up_copy(c).wait_recv()

        if c < comps - LATE_MIX:
            halo_mix(recv_ref, spread_ref, mix_ref, total_ref, c, top)
        if c < comps - LATE_OUT:
            out_ref[c, :half] = out_ref[c, :half] + dot(both_ref[:half], total_ref[c])
            out_ref[c, half:] = out_ref[c, half:] + dot(both_ref[half:], total_ref[c])

    @pl.when(inner)
    def _():
        pair(pl.ds(0, comps), 0).wait_send()

    @pl.when(jnp.logical_not(inner))
    def _():
        pltpu.make_async_remote_copy(
            src_ref=edge_ref.at[0],
            dst_ref=recv_ref.at[0],
            send_sem=send_sem.at[0],
            recv_sem=recv_sem.at[0],
            device_id=(ves, sec),
            device_id_type=MESH,
        ).wait_send()


def finish_kernel(
    part_ref,
    both_ref,
    mix_ref,
    early_ref,
    spread_ref,
    recv_ref,
    out_ref,
    result_ref,
    done_sem,
    piece_sem,
):
    comps, num_points, _ = part_ref.shape
    early = comps - LATE_OUT
    mixed = comps - LATE_MIX
    top = mix_ref.shape[1] - recv_ref.shape[2]
    rows = num_points // PIECES
    stores = [
        pltpu.make_async_copy(part_ref.at[c], out_ref.at[c], done_sem.at[c]) for c in range(early)
    ]
    for store in stores:
        store.start()
    late = []
    for c in range(mixed, comps):
        halo = jnp.concatenate([recv_ref[0, c], recv_ref[1, c]], axis=1)
        upper = (mix_ref[c, :top] + dot(halo[:top], spread_ref[0])).astype(BF16)
        lower = (mix_ref[c, top:] + dot(halo, spread_ref[1])).astype(BF16)
        late.append(jnp.concatenate([upper, lower], axis=0))
    for c in range(early, comps):
        total = early_ref[c] if c < mixed else late[c - mixed]
        for i in range(PIECES):
            part = pl.ds(i * rows, rows)
            result_ref[c - early, part] = part_ref[c, part] + dot(both_ref[part], total)
            store = pltpu.make_async_copy(
                result_ref.at[c - early, part], out_ref.at[c, part], piece_sem.at[c - early, i]
            )
            store.start()
            stores.append(store)
    for store in stores:
        store.wait()


def shards(
    n_ves,
    n_sec,
    density,
    analysis,
    synthesis,
    degree_gain,
    near_kernel,
    partners,
    pair_weight,
    wall_list,
    coupling,
    wall_gain,
):
    count, comps, num_points = density.shape
    num_coefs = analysis.shape[1]
    near_wall = wall_list.shape[0]
    panels, region_wall = coupling.shape
    tile = count // 2
    top = num_coefs // 2 // 16 * 16
    cut = num_coefs - top
    others = max(n_sec - 1, 1)
    vmem = pl.BlockSpec(memory_space=pltpu.VMEM)
    middle = pl.pallas_call(
        functools.partial(step_kernel, n_ves, n_sec),
        name="vesicle_step",
        out_shape=(
            jax.ShapeDtypeStruct((comps, num_points, count), F32),
            jax.ShapeDtypeStruct((num_points, num_coefs), BF16),
            jax.ShapeDtypeStruct((comps, num_coefs, count), F32),
            jax.ShapeDtypeStruct((comps, num_coefs, count), BF16),
            jax.ShapeDtypeStruct((2, 2 * tile, count), BF16),
            jax.ShapeDtypeStruct((2, comps, cut, tile), BF16),
        ),
        in_specs=[pl.BlockSpec(memory_space=pltpu.HBM)] * 10,
        out_specs=[vmem] * 6,
        scratch_shapes=[
            pltpu.VMEM((comps, num_points, count), BF16),
            pltpu.VMEM((num_coefs, num_points), BF16),
            pltpu.VMEM((num_coefs, num_points), BF16),
            pltpu.VMEM((num_points, num_points), BF16),
            pltpu.VMEM(partners.shape[::-1], jnp.int32),
            pltpu.VMEM(partners.shape[::-1], F32),
            pltpu.SMEM((near_wall,), jnp.int32),
            pltpu.VMEM((region_wall, panels), BF16),
            pltpu.VMEM((1, panels), F32),
            pltpu.VMEM((num_coefs,), F32),
            pltpu.VMEM((num_points, num_coefs), BF16),
            pltpu.VMEM((comps, num_coefs, count), BF16),
            pltpu.VMEM((2, comps, cut, tile), BF16),
            pltpu.VMEM((n_sec, comps, near_wall, num_coefs), BF16),
            pltpu.VMEM((others, region_wall, panels), BF16),
            pltpu.VMEM((others, 1, panels), F32),
            pltpu.SemaphoreType.DMA((1,)),
            pltpu.SemaphoreType.DMA((comps,)),
            pltpu.SemaphoreType.DMA((3, others)),
        ],
        compiler_params=pltpu.CompilerParams(
            collective_id=0, has_side_effects=True, vmem_limit_bytes=32 * 1024 * 1024
        ),
    )(
        *(
            pltpu.with_memory_space_constraint(array, pltpu.HBM)
            for array in (
                density.transpose(1, 2, 0),
                analysis.T,
                synthesis,
                degree_gain,
                near_kernel,
                partners.T,
                pair_weight.T,
                wall_list,
                coupling.T,
                wall_gain.reshape(1, panels),
            )
        )
    )
    out = pl.pallas_call(
        finish_kernel,
        name="vesicle_finish",
        out_shape=jax.ShapeDtypeStruct((comps, num_points, count), F32),
        in_specs=[vmem] * 6,
        out_specs=pl.BlockSpec(memory_space=pltpu.HBM),
        scratch_shapes=[
            pltpu.VMEM((LATE_OUT, num_points, count), F32),
            pltpu.SemaphoreType.DMA((comps - LATE_OUT,)),
            pltpu.SemaphoreType.DMA((LATE_OUT, PIECES)),
        ],
        compiler_params=pltpu.CompilerParams(vmem_limit_bytes=16 * 1024 * 1024),
    )(*middle)
    return out.transpose(2, 0, 1)


def solution(mesh):
    n_ves, n_sec = mesh.shape["ves"], mesh.shape["sec"]
    return jax.shard_map(
        functools.partial(shards, n_ves, n_sec),
        mesh=mesh,
        in_specs=(
            P(("ves", "sec"), None, None),
            P(),
            P(),
            P(),
            P(),
            P(("ves", "sec"), None),
            P(("ves", "sec"), None),
            P(("ves", "sec")),
            P(("ves", "sec"), None),
            P(("ves", "sec")),
        ),
        out_specs=P(("ves", "sec"), None, None),
        check_vma=False,
    )
```
